128 devices in a mesh: grp: 8 (over x_hi, y), mem: 16 (over x_lo, z, core).
Axes of the slice: x: 4 (x_hi: 2, x_lo: 2; x = x_hi * 2 + x_lo), y: 4, z: 4, core: 2. Of those that a mesh axis runs over, the one named last changes fastest.
Arguments:
- activations: bfloat16 [4096, 32, 4096], P(('grp', 'mem')), may hold values from -6 to 6
- out_grads: bfloat16 [4096, 32, 4096], P(('grp', 'mem')), may hold values from -6 to 6
- proj_in: bfloat16 [4096, 64], replicated, may hold values from -1 to 1
- proj_out: bfloat16 [4096, 64], replicated, may hold values from -1 to 1
- basis_in: float32 [64, 64], replicated, may hold values from -1 to 1
- basis_out: float32 [64, 64], replicated, may hold values from -1 to 1
- eigen: float32 [64, 64], replicated, may hold values from 0.05 to 12
- doc_ids: int32 [4096], P(('grp', 'mem')), may hold values from 0 to 1023
Outputs:
- scores: float32 [4096, 4096], P(('grp', 'mem'))
The draws below stay inside these ranges and needn't reach their ends.
All inputs are finite; a program needn't handle non-finite values.
Results may differ from the reference program's by a relative error of at most 0.0077.
Values may be sent and summed in bfloat16 or wider, within the bound.
A program may use at most 192 MiB of HBM per device.

```python
import math
import jax
import jax.numpy as jnp
from jax import lax

D = 4096
R = 64
TOK_EX = 32
E_DEV = 32
EXAMPLES = 4096


def ekfac_common(key):
    key_list = [jax.random.fold_in(key, 7001 + offset) for offset in range(8)]
    basis_in = jnp.linalg.qr(jax.random.normal(key_list[0], (R, R), jnp.float32))[0]
    basis_out = jnp.linalg.qr(jax.random.normal(key_list[1], (R, R), jnp.float32))[0]
    proj_in = jnp.clip(jax.random.normal(key_list[2], (D, R), jnp.float32), -5.0, 5.0) / math.sqrt(D)
    proj_out = jnp.clip(jax.random.normal(key_list[3], (D, R), jnp.float32), -5.0, 5.0) / math.sqrt(D)
    proj_in = proj_in.astype(jnp.bfloat16).astype(jnp.float32)
    proj_out = proj_out.astype(jnp.bfloat16).astype(jnp.float32)
    target_in = jnp.exp(jax.random.uniform(key_list[4], (R,), jnp.float32, math.log(0.3), math.log(3.0)))
    target_out = jnp.exp(jax.random.uniform(key_list[5], (R,), jnp.float32, math.log(0.3), math.log(3.0)))
    correction = jnp.exp(jax.random.uniform(key_list[6], (R, R), jnp.float32, math.log(0.8), math.log(1.25)))
    return (basis_in, basis_out, proj_in, proj_out, target_in, target_out, correction)


def side_map(projection, eigenbasis):
    high = lax.Precision.HIGHEST
    mapped = jnp.dot(projection, eigenbasis, precision=high)
    gram_matrix = jnp.dot(mapped.T, mapped, precision=high)
    lift_map = jnp.linalg.solve(gram_matrix, mapped.T)
    return (lift_map, jnp.diagonal(gram_matrix))


def side_variance(projection, eigenbasis, target):
    lift_map, gram_diag = side_map(projection, eigenbasis)
    return 0.25 * gram_diag + target - 0.25


def logged_rows(key, projection, eigenbasis, target, salt_value):
    lift_map, gram_diag = side_map(projection, eigenbasis)
    spread = jnp.sqrt(target - 0.25)
    base_key = jax.random.fold_in(key, salt_value)

    def block_rows(position):
        block_key = jax.random.fold_in(base_key, position)
        noise_key, coeff_key = jax.random.split(block_key)
        noise_part = jax.random.normal(noise_key, (E_DEV, TOK_EX, D), jnp.float32)
        coeffs = jax.random.normal(coeff_key, (E_DEV, TOK_EX, R), jnp.float32)
        row_block = 0.5 * noise_part + jnp.einsum('etk,kd->etd', coeffs * spread, lift_map)
        return jnp.clip(row_block, -6.0, 6.0).astype(jnp.bfloat16)
    stacked = lax.map(block_rows, jnp.arange(EXAMPLES // E_DEV, dtype=jnp.int32))
    return stacked.reshape(EXAMPLES, TOK_EX, D)


def draw_activations(key, part):
    basis_in, basis_out, proj_in, proj_out, target_in, target_out, correction = ekfac_common(key)
    return logged_rows(key, proj_in, basis_in, target_in, 8101)


def draw_out_grads(key, part):
    basis_in, basis_out, proj_in, proj_out, target_in, target_out, correction = ekfac_common(key)
    return logged_rows(key, proj_out, basis_out, target_out, 8202)


def draw_proj_in(key, part):
    common = ekfac_common(key)
    return common[2].astype(jnp.bfloat16)


def draw_proj_out(key, part):
    common = ekfac_common(key)
    return common[3].astype(jnp.bfloat16)


def draw_basis_in(key, part):
    common = ekfac_common(key)
    return common[0]


def draw_basis_out(key, part):
    common = ekfac_common(key)
    return common[1]


def draw_eigen(key, part):
    basis_in, basis_out, proj_in, proj_out, target_in, target_out, correction = ekfac_common(key)
    input_var = side_variance(proj_in, basis_in, target_in)
    output_var = side_variance(proj_out, basis_out, target_out)
    measured = output_var[:, None] * input_var[None, :] * correction
    return jnp.clip(measured, 0.05, 12.0)


def plant(values, own_key, least, top_value):
    spot = [jax.random.randint(jax.random.fold_in(own_key, axis), (), 0, length) for axis, length in enumerate(values.shape)]
    longest = values.shape.index(max(values.shape))
    neighbour = spot[:longest] + [(spot[longest] + 1) % values.shape[longest]] + spot[longest + 1:]
    return values.at[tuple(spot)].set(least).at[tuple(neighbour)].set(top_value)


def setup_inputs(seed: int = 0) -> dict:
    splits = jax.random.split(jax.random.key(seed), 9)
    return {
        "activations": draw_activations(jax.random.fold_in(splits[8], 71), 0),
        "out_grads": draw_out_grads(jax.random.fold_in(splits[8], 71), 0),
        "proj_in": draw_proj_in(jax.random.fold_in(splits[8], 71), 0),
        "proj_out": draw_proj_out(jax.random.fold_in(splits[8], 71), 0),
        "basis_in": draw_basis_in(jax.random.fold_in(splits[8], 71), 0),
        "basis_out": draw_basis_out(jax.random.fold_in(splits[8], 71), 0),
        "eigen": draw_eigen(jax.random.fold_in(splits[8], 71), 0),
        "doc_ids": plant(jax.random.randint(splits[7], (EXAMPLES,), 0, EXAMPLES // 4), jax.random.fold_in(splits[7], 1), 0, (EXAMPLES // 4) - 1).astype(jnp.int32),
    }


damping = 0.1

def reference(activations, out_grads, proj_in, proj_out, basis_in, basis_out, eigen, doc_ids):
    high = lax.Precision.HIGHEST
    blocks = EXAMPLES // E_DEV

    def features(pair):
        act_block, grad_block = pair
        act_proj = jnp.dot(act_block.reshape(-1, D).astype(jnp.float32), proj_in.astype(jnp.float32), preferred_element_type=jnp.float32).astype(jnp.bfloat16)
        grad_proj = jnp.dot(grad_block.reshape(-1, D).astype(jnp.float32), proj_out.astype(jnp.float32), preferred_element_type=jnp.float32).astype(jnp.bfloat16)
        act_proj = act_proj.reshape(E_DEV, TOK_EX, R).astype(jnp.float32)
        grad_proj = grad_proj.reshape(E_DEV, TOK_EX, R).astype(jnp.float32)
        grad_feat = jnp.einsum('etr,ets->ers', grad_proj, act_proj, precision=high)
        rotated = jnp.einsum('ers,ru->eus', grad_feat, basis_out, precision=high)
        rotated = jnp.einsum('eus,sv->euv', rotated, basis_in, precision=high)
        return (rotated / jnp.sqrt(eigen + damping)).astype(jnp.bfloat16).reshape(E_DEV, R * R)
    scaled = lax.map(features, (activations.reshape(blocks, E_DEV, TOK_EX, D), out_grads.reshape(blocks, E_DEV, TOK_EX, D)))
    scaled = scaled.reshape(EXAMPLES, R * R).astype(jnp.float32)
    products = jnp.dot(scaled, scaled.T, precision=high)
    products = products * (1.0 / (TOK_EX * R))
    same_doc = doc_ids[:, None] == doc_ids[None, :]
    return jnp.where(same_doc, jnp.float32(0.0), products)
```

```python
import functools

import jax
import jax.numpy as jnp
from jax import lax
from jax.experimental import pallas as pl
from jax.experimental.pallas import tpu as pltpu
from jax.sharding import PartitionSpec as P

damping = 0.1
BF = jnp.bfloat16
F32 = jnp.float32
MESH = pl.DeviceIdType.MESH
NT = (((1,), (1,)), ((), ()))


def dot(a, b):
    return jnp.dot(a, b, preferred_element_type=F32)


def split(value):
    high = value.astype(BF)
    return high, (value - high.astype(F32)).astype(BF)


def feature_kernel(
    act_hbm, grad_hbm, pin_hbm, pout_hbm, bin_ref, bout_ref, eig_ref, out_ref,
    act, grad, w_in, w_out, w_g, scale, dsem, wsem,
):
    copies = []
    for part in range(4):
        rows = pl.ds(part * 256, 256)
        copies.append(
            (
                pltpu.make_async_copy(act_hbm.at[rows], act.at[rows], dsem.at[part]),
                pltpu.make_async_copy(grad_hbm.at[rows], grad.at[rows], dsem.at[4 + part]),
            )
        )
    weights = (
        pltpu.make_async_copy(pin_hbm, w_in.at[pl.ds(0, 64)], wsem.at[0]),
        pltpu.make_async_copy(pout_hbm, w_out.at[pl.ds(64, 64)], wsem.at[1]),
    )
    for copy in weights:
        copy.start()
    for pair in copies:
        for copy in pair:
            copy.start()
    w_in[64:, :] = jnp.zeros((64, 4096), BF)
    w_out[:64, :] = jnp.zeros((64, 4096), BF)

    zeros = jnp.zeros((64, 64), BF)
    out_high, out_low = split(bout_ref[...])
    stacked = jnp.concatenate([zeros, out_high, zeros, out_low], axis=0)
    for tile in range(16):
        unit = lax.broadcasted_iota(jnp.int32, (64, 256), 0)
        lane = lax.broadcasted_iota(jnp.int32, (64, 256), 1)
        spread = jnp.where(lax.div(lane, 64) + tile * 4 == unit, 1.0, 0.0).astype(BF)
        w_g[:, tile * 256 : (tile + 1) * 256] = dot(stacked, spread).astype(BF)
    in_high, in_low = split(bin_ref[...])
    wide_zeros = jnp.zeros((64, 128), BF)
    w_a = jnp.concatenate(
        [
            jnp.concatenate([in_high, in_high], axis=1),
            wide_zeros,
            jnp.concatenate([in_low, in_low], axis=1),
            wide_zeros,
        ],
        axis=0,
    )
    inverse = 1.0 / jnp.sqrt(eig_ref[...] + damping)
    for tile in range(32):
        scale[:, tile * 128 : (tile + 1) * 128] = jnp.concatenate(
            [inverse[2 * tile : 2 * tile + 1], inverse[2 * tile + 1 : 2 * tile + 2]], axis=1
        )
    row = lax.broadcasted_iota(jnp.int32, (256, 256), 0)
    col = lax.broadcasted_iota(jnp.int32, (256, 256), 1)
    perm = jnp.where(lax.rem(row, 8) * 32 + lax.div(row, 8) == col, 1.0, 0.0).astype(BF)

    for copy in weights:
        copy.wait()
    for half in range(2):
        both, twice = [], []
        for sub in range(2):
            part = half * 2 + sub
            for copy in copies[part]:
                copy.wait()
            rows = pl.ds(part * 256, 256)
            projected = lax.dot_general(
                act[rows, :], w_in[...], NT, preferred_element_type=F32
            ) + lax.dot_general(grad[rows, :], w_out[...], NT, preferred_element_type=F32)
            moved = dot(perm, projected.astype(BF)).astype(BF)
            pair = jnp.concatenate([moved, moved], axis=1)
            rotated = dot(pair, w_a)
            both.append(pair)
            twice.append(jnp.concatenate([rotated, rotated], axis=1))
        for tile in range(16):
            lanes = slice(tile * 256, (tile + 1) * 256)
            sums = []
            for sub in range(2):
                product = dot(both[sub], w_g[:, lanes]) * twice[sub]
                sums.append(jnp.sum(product.reshape(32, 8, 256), axis=0))
            out_ref[half, :, lanes] = (
                jnp.concatenate(sums, axis=0) * scale[:, lanes]
            ).astype(BF)


def features(act, grad, pin, pout, basis_in, basis_out, eigen):
    vmem = pl.BlockSpec(memory_space=pltpu.VMEM)
    hbm = pl.BlockSpec(memory_space=pl.ANY)
    return pl.pallas_call(
        feature_kernel,
        out_shape=jax.ShapeDtypeStruct((2, 16, 4096), BF),
        in_specs=[hbm] * 4 + [vmem] * 3,
        out_specs=vmem,
        scratch_shapes=[
            pltpu.VMEM((1024, 4096), BF),
            pltpu.VMEM((1024, 4096), BF),
            pltpu.VMEM((128, 4096), BF),
            pltpu.VMEM((128, 4096), BF),
            pltpu.VMEM((256, 4096), BF),
            pltpu.VMEM((1, 4096), F32),
            pltpu.SemaphoreType.DMA((8,)),
            pltpu.SemaphoreType.DMA((2,)),
        ],
        compiler_params=pltpu.CompilerParams(vmem_limit_bytes=60 << 20),
        name="features",
    )(act, grad, pin, pout, basis_in, basis_out, eigen)


def score_kernel(
    feat_hbm, ids_ref, out_ref,
    rowbuf, colbuf, res_send, res_recv, id_col, id_row, row_ids, col_ids,
    lsem, ssem, rsem, isend, irecv, osend, orecv,
    *, factor,
):
    g = lax.axis_index("grp")
    m = lax.axis_index("mem")
    x = lax.div(g, 4) * 2 + lax.div(m, 8)
    y = lax.rem(g, 4)
    z = lax.rem(lax.div(m, 2), 4)
    c = lax.rem(m, 2)
    odd = lax.rem(z, 2)
    zr = lax.rem(z + 3 + 2 * odd, 4)
    zc = z + 1 - 2 * odd
    xm, xp, x2 = lax.rem(x + 3, 4), lax.rem(x + 1, 4), lax.rem(x + 2, 4)
    ym, yp, y2 = lax.rem(y + 3, 4), lax.rem(y + 1, 4), lax.rem(y + 2, 4)
    oc = 1 - c

    def device(x, y, z, c):
        return (lax.div(x, 2) * 4 + y, lax.rem(x, 2) * 8 + z * 2 + c)

    def slot(y, z, c):
        return y * 4 + lax.rem(z, 2) * 2 + c

    row_places = [(a, b) for b in (z, zr) for a in (x, xm, xp, x2)]
    row_peers = [device(a, y, b, c) for a, b in row_places[1:]]
    col_places = [(a, b) for b in (z, zc) for a in (y, ym, yp, y2)]
    col_peers = [device(x, a, b, c) for a, b in col_places[1:]]
    cross_peers = [device(x, a, b, oc) for a, b in col_places]

    local = [
        pltpu.make_async_copy(feat_hbm, rowbuf.at[0], lsem.at[0]),
        pltpu.make_async_copy(feat_hbm, colbuf.at[slot(y, z, c)], lsem.at[1]),
    ]
    for copy in local:
        copy.start()
    barrier = pltpu.get_barrier_semaphore()
    everyone = row_peers + col_peers + cross_peers
    for peer in everyone:
        pl.semaphore_signal(barrier, inc=1, device_id=peer, device_id_type=MESH)

    lane = lax.broadcasted_iota(jnp.int32, (8, 128), 1)
    first = (odd * 2 + c) * 32
    placed = jnp.zeros((8, 128), jnp.int32)
    for example in range(32):
        value = ids_ref[example]
        placed = jnp.where(lane == first + example, value, placed)
        id_col[example : example + 1, :] = jnp.full((1, 128), value, jnp.int32)
    id_row[...] = placed
    row_ids[0] = id_col[...]
    col_ids[slot(y, z, c)] = placed

    for copy in local:
        copy.wait()
    pl.semaphore_wait(barrier, len(everyone))

    started = []

    def send(src, dst, send_sem, recv_sem, peer):
        copy = pltpu.make_async_remote_copy(
            src_ref=src, dst_ref=dst, send_sem=send_sem, recv_sem=recv_sem,
            device_id=peer, device_id_type=MESH,
        )
        copy.start()
        started.append(copy)

    own = slot(y, z, c)
    to = {
        "x+": device(xp, y, z, c), "x-": device(xm, y, z, c),
        "y+": device(x, yp, z, c), "y-": device(x, ym, z, c),
        "zr": device(x, y, zr, c), "zc": device(x, y, zc, c),
        "core": device(x, y, z, oc),
    }
    count = [0]

    def piece(src, dst, number, where):
        send(src, dst, ssem.at[count[0]], rsem.at[number], to[where])
        count[0] += 1

    def row(k, half):
        return rowbuf.at[k, half]

    def col(index, half):
        return colbuf.at[index, half]

    def row_number(k, half):
        return (k - 1) * 2 + half

    col_names = ["own", "ym", "yp", "y2", "zc", "zcym", "zcyp", "zcy2"]

    def col_number(name, half):
        return 14 + (col_names.index(name) - 1) * 2 + half

    def cross_number(name, half):
        return 28 + col_names.index(name) * 2 + half

    slots = {name: slot(a, b, c) for name, (a, b) in zip(col_names, col_places)}
    other = {name: slot(a, b, oc) for name, (a, b) in zip(col_names, col_places)}

    def row_wait(k, half):
        ref = row(k, half)
        pltpu.make_async_copy(ref, ref, rsem.at[row_number(k, half)]).wait()

    def col_wait(name, half):
        ref = col(slots[name], half)
        pltpu.make_async_copy(ref, ref, rsem.at[col_number(name, half)]).wait()

    def cross_wait(name, half):
        ref = col(other[name], half)
        pltpu.make_async_copy(ref, ref, rsem.at[cross_number(name, half)]).wait()

    def row_send(k, half, where, lands):
        piece(row(k, half), row(lands, half), row_number(lands, half), where)

    def col_send(name, half, where, lands):
        ref = col(slots[name], half)
        piece(ref, ref, col_number(lands, half), where)

    def cross_send(name, half):
        ref = col(slots[name], half)
        piece(ref, ref, cross_number(name, half), "core")

    mirror = [0, 2, 1, 3, 4, 6, 5, 7]
    for k, peer in enumerate(row_peers, 1):
        at = mirror[k]
        send(id_col, row_ids.at[at], isend.at[k - 1], irecv.at[at - 1], peer)
    for k, peer in enumerate(col_peers, 1):
        send(id_row, col_ids.at[own], isend.at[6 + k], irecv.at[6 + mirror[k]], peer)
    for k, peer in enumerate(cross_peers):
        send(id_row, col_ids.at[own], isend.at[14 + k], irecv.at[14 + mirror[k]], peer)

    for half in range(2):
        row_send(0, half, "zr", 4)
        col_send("own", half, "zc", "zc")
        row_send(0, half, "x+", 1)
        row_send(0, half, "x-", 2)
        col_send("own", half, "y+", "ym")
        col_send("own", half, "y-", "yp")
        cross_send("own", half)
    for half in range(2):
        row_wait(4, half)
        row_send(4, half, "x+", 5)
        row_send(4, half, "x-", 6)
        col_wait("zc", half)
        col_send("zc", half, "y+", "zcym")
        col_send("zc", half, "y-", "zcyp")
        cross_send("zc", half)
    row_wait(1, 0)
    row_send(1, 0, "x+", 3)
    row_wait(2, 0)
    col_wait("ym", 0)
    col_send("ym", 0, "y+", "y2")
    cross_send("ym", 0)
    col_wait("yp", 0)
    cross_send("yp", 0)
    row_wait(2, 1)
    row_send(2, 1, "x-", 3)
    row_wait(1, 1)
    col_wait("yp", 1)
    col_send("yp", 1, "y-", "y2")
    cross_send("yp", 1)
    col_wait("ym", 1)
    cross_send("ym", 1)
    for half in range(2):
        for k in (5, 6):
            row_wait(k, half)
        for name in ("zcym", "zcyp"):
            col_wait(name, half)
            cross_send(name, half)
    for half in range(2):
        row_wait(3, half)
        row_send(3, half, "zr", 7)
        col_wait("y2", half)
        col_send("y2", half, "zc", "zcy2")
        cross_send("y2", half)
    for half in range(2):
        col_wait("zcy2", half)
        cross_send("zcy2", half)
        row_wait(7, half)

    for number in range(7):
        ref = row_ids.at[number + 1]
        pltpu.make_async_copy(ref, ref, irecv.at[number]).wait()
    for number, name in enumerate(col_names[1:]):
        ref = col_ids.at[slots[name]]
        pltpu.make_async_copy(ref, ref, irecv.at[7 + number]).wait()
    for number, name in enumerate(col_names):
        ref = col_ids.at[other[name]]
        pltpu.make_async_copy(ref, ref, irecv.at[14 + number]).wait()
    for name in col_names:
        for half in range(2):
            cross_wait(name, half)

    mine = x * 2 + lax.div(z, 2)

    def score(tile, carry):
        block = pl.ds(tile * 4, 4)
        products = lax.dot_general(
            rowbuf[...].reshape(256, 4096),
            colbuf[block].reshape(128, 4096),
            NT,
            preferred_element_type=F32,
        )
        ids = jnp.sum(col_ids[block], axis=0)[:1]
        for k in range(8):
            part = products[k * 32 : (k + 1) * 32] * factor
            part = jnp.where(row_ids[k] == ids, 0.0, part).astype(BF)
            res_send[k, :, pl.ds(pl.multiple_of(tile * 128, 128), 128)] = part
        return carry

    lax.fori_loop(0, 4, score, 0)
    for k, peer in enumerate(row_peers, 1):
        at = mirror[k] - 1
        send(res_send.at[k], res_recv.at[mine], osend.at[k - 1], orecv.at[at], peer)
    res_recv[mine] = res_send[0]
    for number in range(7):
        a, b = row_places[number + 1]
        ref = res_recv.at[a * 2 + lax.div(b, 2)]
        pltpu.make_async_copy(ref, ref, orecv.at[number]).wait()
    for index in range(8):
        xi, k = index // 2, index % 2
        for yi in range(4):
            at = (xi // 2) * 2048 + yi * 512 + (xi % 2) * 256 + k * 128
            out_ref[:, at : at + 128] = res_recv[index, :, yi * 128 : (yi + 1) * 128].astype(F32)
    for copy in started:
        copy.wait_send()


def scores(feat, ids, factor):
    return pl.pallas_call(
        functools.partial(score_kernel, factor=factor),
        out_shape=jax.ShapeDtypeStruct((32, 4096), F32),
        in_specs=[pl.BlockSpec(memory_space=pl.ANY), pl.BlockSpec(memory_space=pltpu.SMEM)],
        out_specs=pl.BlockSpec(memory_space=pltpu.VMEM),
        scratch_shapes=[
            pltpu.VMEM((8, 2, 16, 4096), BF),
            pltpu.VMEM((16, 2, 16, 4096), BF),
            pltpu.VMEM((8, 32, 512), BF),
            pltpu.VMEM((8, 32, 512), BF),
            pltpu.VMEM((32, 128), jnp.int32),
            pltpu.VMEM((8, 128), jnp.int32),
            pltpu.VMEM((8, 32, 128), jnp.int32),
            pltpu.VMEM((16, 8, 128), jnp.int32),
            pltpu.SemaphoreType.DMA((2,)),
            pltpu.SemaphoreType.DMA((44,)),
            pltpu.SemaphoreType.DMA((44,)),
            pltpu.SemaphoreType.DMA((22,)),
            pltpu.SemaphoreType.DMA((22,)),
            pltpu.SemaphoreType.DMA((7,)),
            pltpu.SemaphoreType.DMA((7,)),
        ],
        compiler_params=pltpu.CompilerParams(
            collective_id=0, has_side_effects=True, vmem_limit_bytes=48 << 20
        ),
        name="scores",
    )(feat, ids)


def on_device(activations, out_grads, proj_in, proj_out, basis_in, basis_out, eigen, doc_ids):
    local_count, tokens, width = activations.shape
    rank = proj_in.shape[1]
    feat = features(
        activations.reshape(-1, width), out_grads.reshape(-1, width),
        proj_in.T, proj_out.T, basis_in, basis_out, eigen,
    )
    return scores(feat, doc_ids, 1.0 / (tokens * rank))


def solution(mesh):
    return jax.shard_map(
        on_device,
        mesh=mesh,
        in_specs=(
            P(("grp", "mem"), None, None),
            P(("grp", "mem"), None, None),
            P(),
            P(),
            P(),
            P(),
            P(),
            P(("grp", "mem")),
        ),
        out_specs=P(("grp", "mem"), None),
        check_vma=False,
    )
```

```python
import functools

import jax
import jax.numpy as jnp
from jax import lax
from jax.experimental import pallas as pl
from jax.experimental.pallas import tpu as pltpu
from jax.sharding import PartitionSpec as P

damping = 0.1
BF = jnp.bfloat16
F32 = jnp.float32
MESH = pl.DeviceIdType.MESH
NT = (((1,), (1,)), ((), ()))


def dot(a, b):
    return jnp.dot(a, b, preferred_element_type=F32)


def split(value):
    high = value.astype(BF)
    return high, (value - high.astype(F32)).astype(BF)


def kernel(
    act_hbm, grad_hbm, pin_hbm, pout_hbm, bin_hbm, bout_hbm, eig_hbm, ids_hbm, out_ref,
    act, grad, w_in, w_out, b_in, b_out, eig, ids_ref, w_g, scale,
    rowbuf, colbuf, res_send, res_recv, id_col, id_row, row_ids, col_ids,
    dsem, wsem, ssem, rsem, isend, irecv, osend, orecv,
    *, factor,
):
    g = lax.axis_index("grp")
    m = lax.axis_index("mem")
    x = lax.div(g, 4) * 2 + lax.div(m, 8)
    y = lax.rem(g, 4)
    z = lax.rem(lax.div(m, 2), 4)
    c = lax.rem(m, 2)
    odd = lax.rem(z, 2)
    zr = lax.rem(z + 3 + 2 * odd, 4)
    zc = z + 1 - 2 * odd
    xm, xp, x2 = lax.rem(x + 3, 4), lax.rem(x + 1, 4), lax.rem(x + 2, 4)
    ym, yp, y2 = lax.rem(y + 3, 4), lax.rem(y + 1, 4), lax.rem(y + 2, 4)
    oc = 1 - c

    def device(x, y, z, c):
        return (lax.div(x, 2) * 4 + y, lax.rem(x, 2) * 8 + z * 2 + c)

    def slot(y, z, c):
        return y * 4 + lax.rem(z, 2) * 2 + c

    row_places = [(a, b) for b in (z, zr) for a in (x, xm, xp, x2)]
    row_peers = [device(a, y, b, c) for a, b in row_places[1:]]
    col_places = [(a, b) for b in (z, zc) for a in (y, ym, yp, y2)]
    col_peers = [device(x, a, b, c) for a, b in col_places[1:]]
    cross_peers = [device(x, a, b, oc) for a, b in col_places]
    own = slot(y, z, c)

    weights = [
        pltpu.make_async_copy(src, dst, wsem.at[number])
        for number, (src, dst) in enumerate(
            [
                (bout_hbm, b_out), (bin_hbm, b_in), (eig_hbm, eig), (ids_hbm, ids_ref),
                (pin_hbm, w_in), (pout_hbm, w_out),
            ]
        )
    ]
    loads = []
    for part in range(4):
        rows = pl.ds(part * 256, 256)
        loads.append(
            (
                pltpu.make_async_copy(act_hbm.at[rows], act.at[rows], dsem.at[part]),
                pltpu.make_async_copy(grad_hbm.at[rows], grad.at[rows], dsem.at[4 + part]),
            )
        )
    for copy in weights:
        copy.start()
    for part in range(2):
        for copy in loads[part]:
            copy.start()
    barrier = pltpu.get_barrier_semaphore()
    everyone = row_peers + col_peers + cross_peers
    for peer in everyone:
        pl.semaphore_signal(barrier, inc=1, device_id=peer, device_id_type=MESH)

    for copy in weights[:4]:
        copy.wait()
    zeros = jnp.zeros((64, 64), BF)
    out_high, out_low = split(b_out[...])
    stacked = jnp.concatenate([zeros, out_high, zeros, out_low], axis=0)
    for tile in range(16):
        unit = lax.broadcasted_iota(jnp.int32, (64, 256), 0)
        lane = lax.broadcasted_iota(jnp.int32, (64, 256), 1)
        spread = jnp.where(lax.div(lane, 64) + tile * 4 == unit, 1.0, 0.0).astype(BF)
        w_g[:, tile * 256 : (tile + 1) * 256] = dot(stacked, spread).astype(BF)
    in_high, in_low = split(b_in[...])
    wide_zeros = jnp.zeros((64, 128), BF)
    w_a = jnp.concatenate(
        [
            jnp.concatenate([in_high, in_high], axis=1),
            wide_zeros,
            jnp.concatenate([in_low, in_low], axis=1),
            wide_zeros,
        ],
        axis=0,
    )
    inverse = 1.0 / jnp.sqrt(eig[...] + damping)
    for tile in range(32):
        scale[:, tile * 128 : (tile + 1) * 128] = jnp.concatenate(
            [inverse[2 * tile : 2 * tile + 1], inverse[2 * tile + 1 : 2 * tile + 2]], axis=1
        )
    row_at = lax.broadcasted_iota(jnp.int32, (256, 256), 0)
    col_at = lax.broadcasted_iota(jnp.int32, (256, 256), 1)
    perm = jnp.where(
        lax.rem(row_at, 8) * 32 + lax.div(row_at, 8) == col_at, 1.0, 0.0
    ).astype(BF)

    lane = lax.broadcasted_iota(jnp.int32, (8, 128), 1)
    first = (odd * 2 + c) * 32
    placed = jnp.zeros((8, 128), jnp.int32)
    for example in range(32):
        value = ids_ref[example]
        placed = jnp.where(lane == first + example, value, placed)
        id_col[example : example + 1, :] = jnp.full((1, 128), value, jnp.int32)
    id_row[...] = placed
    row_ids[0] = id_col[...]
    col_ids[own] = placed

    started = []

    def send(src, dst, send_sem, recv_sem, peer):
        copy = pltpu.make_async_remote_copy(
            src_ref=src, dst_ref=dst, send_sem=send_sem, recv_sem=recv_sem,
            device_id=peer, device_id_type=MESH,
        )
        copy.start()
        started.append(copy)

    to = {
        "x+": device(xp, y, z, c), "x-": device(xm, y, z, c),
        "y+": device(x, yp, z, c), "y-": device(x, ym, z, c),
        "zr": device(x, y, zr, c), "zc": device(x, y, zc, c),
        "core": device(x, y, z, oc),
    }
    count = [0]

    def piece(src, dst, number, where):
        send(src, dst, ssem.at[count[0]], rsem.at[number], to[where])
        count[0] += 1

    def row(k, q):
        return rowbuf.at[k, pl.ds(q * 8, 8)]

    def col(index, q):
        return colbuf.at[index, pl.ds(q * 8, 8)]

    col_names = ["own", "ym", "yp", "y2", "zc", "zcym", "zcyp", "zcy2"]
    row_names = ["own", "xm", "xp", "x2", "zr", "zrxm", "zrxp", "zrx2"]

    def row_number(name, q):
        return (row_names.index(name) - 1) * 4 + q

    def col_number(name, q):
        return 28 + (col_names.index(name) - 1) * 4 + q

    def cross_number(name, q):
        return 56 + col_names.index(name) * 4 + q

    slots = {name: slot(a, b, c) for name, (a, b) in zip(col_names, col_places)}
    other = {name: slot(a, b, oc) for name, (a, b) in zip(col_names, col_places)}

    def row_wait(name, q):
        ref = row(row_names.index(name), q)
        pltpu.make_async_copy(ref, ref, rsem.at[row_number(name, q)]).wait()

    def col_wait(name, q):
        ref = col(slots[name], q)
        pltpu.make_async_copy(ref, ref, rsem.at[col_number(name, q)]).wait()

    def cross_wait(name, q):
        ref = col(other[name], q)
        pltpu.make_async_copy(ref, ref, rsem.at[cross_number(name, q)]).wait()

    def row_send(name, q, where, lands):
        src, dst = row(row_names.index(name), q), row(row_names.index(lands), q)
        piece(src, dst, row_number(lands, q), where)

    def col_send(name, q, where, lands):
        ref = col(slots[name], q)
        piece(ref, ref, col_number(lands, q), where)

    def cross_send(name, q):
        ref = col(slots[name], q)
        piece(ref, ref, cross_number(name, q), "core")

    def own_out(q):
        row_send("own", q, "zr", "zr")
        col_send("own", q, "zc", "zc")
        row_send("own", q, "x+", "xm")
        row_send("own", q, "x-", "xp")
        col_send("own", q, "y+", "ym")
        col_send("own", q, "y-", "yp")
        cross_send("own", q)

    def z_on(q):
        row_wait("zr", q)
        row_send("zr", q, "x+", "zrxm")
        row_send("zr", q, "x-", "zrxp")
        col_wait("zc", q)
        col_send("zc", q, "y+", "zcym")
        col_send("zc", q, "y-", "zcyp")
        cross_send("zc", q)

    def far_on(q):
        row_wait("xm", q)
        row_wait("xp", q)
        if q < 2:
            row_send("xm", q, "x+", "x2")
        else:
            row_send("xp", q, "x-", "x2")
        col_wait("ym", q)
        col_wait("yp", q)
        if q < 2:
            col_send("ym", q, "y+", "y2")
        else:
            col_send("yp", q, "y-", "y2")
        cross_send("ym", q)
        cross_send("yp", q)

    mirror = [0, 2, 1, 3, 4, 6, 5, 7]
    for copy in weights[4:]:
        copy.wait()
    for part in range(4):
        for copy in loads[part]:
            copy.wait()
        if part < 2:
            for copy in loads[part + 2]:
                copy.start()
        rows = pl.ds(part * 256, 256)
        projected = jnp.concatenate(
            [
                lax.dot_general(act[rows, :], w_in[...], NT, preferred_element_type=F32),
                lax.dot_general(grad[rows, :], w_out[...], NT, preferred_element_type=F32),
            ],
            axis=1,
        )
        moved = dot(perm, projected.astype(BF)).astype(BF)
        pair = jnp.concatenate([moved, moved], axis=1)
        rotated = dot(pair, w_a)
        twice = jnp.concatenate([rotated, rotated], axis=1)
        for tile in range(16):
            lanes = slice(tile * 256, (tile + 1) * 256)
            product = dot(pair, w_g[:, lanes]) * twice
            feature = jnp.sum(product.reshape(32, 8, 256), axis=0) * scale[:, lanes]
            feature = feature.astype(BF)
            rowbuf[0, part * 8 : (part + 1) * 8, lanes] = feature
            colbuf[own, part * 8 : (part + 1) * 8, lanes] = feature
        if part == 0:
            pl.semaphore_wait(barrier, len(everyone))
            for k, peer in enumerate(row_peers, 1):
                at = mirror[k]
                send(id_col, row_ids.at[at], isend.at[k - 1], irecv.at[at - 1], peer)
            for k, peer in enumerate(col_peers, 1):
                send(id_row, col_ids.at[own], isend.at[6 + k], irecv.at[6 + mirror[k]], peer)
            for k, peer in enumerate(cross_peers):
                send(id_row, col_ids.at[own], isend.at[14 + k], irecv.at[14 + mirror[k]], peer)
        else:
            z_on(part - 1)
        own_out(part)
        if part >= 2:
            far_on(part - 2)
    z_on(3)
    far_on(2)
    far_on(3)
    for q in range(4):
        for name in ("zcym", "zcyp"):
            col_wait(name, q)
            cross_send(name, q)
        for name in ("zrxm", "zrxp"):
            row_wait(name, q)
    for q in (0, 2, 1, 3):
        row_wait("x2", q)
        row_send("x2", q, "zr", "zrx2")
        col_wait("y2", q)
        col_send("y2", q, "zc", "zcy2")
        cross_send("y2", q)
    for q in (0, 2, 1, 3):
        col_wait("zcy2", q)
        cross_send("zcy2", q)
        row_wait("zrx2", q)

    for k in range(1, 8):
        ref = row_ids.at[k]
        pltpu.make_async_copy(ref, ref, irecv.at[k - 1]).wait()
    for k, name in enumerate(col_names):
        if k:
            ref = col_ids.at[slots[name]]
            pltpu.make_async_copy(ref, ref, irecv.at[6 + k]).wait()
        ref = col_ids.at[other[name]]
        pltpu.make_async_copy(ref, ref, irecv.at[14 + k]).wait()
    for name in col_names:
        for q in range(4):
            cross_wait(name, q)

    mine = x * 2 + lax.div(z, 2)
    for half in range(2):
        block = pl.ds(half * 8, 8)
        products = lax.dot_general(
            rowbuf[...].reshape(256, 4096),
            colbuf[block].reshape(256, 4096),
            NT,
            preferred_element_type=F32,
        )
        ids = jnp.concatenate(
            [
                jnp.sum(col_ids[pl.ds(half * 8 + 4 * part, 4)], axis=0)[:1]
                for part in range(2)
            ],
            axis=1,
        )
        for k in range(8):
            part = products[k * 32 : (k + 1) * 32] * factor
            same = jnp.concatenate([row_ids[k], row_ids[k]], axis=1) == ids
            res_send[k, :, half * 256 : (half + 1) * 256] = jnp.where(same, 0.0, part).astype(BF)
    for k, peer in enumerate(row_peers, 1):
        at = mirror[k] - 1
        send(res_send.at[k], res_recv.at[mine], osend.at[k - 1], orecv.at[at], peer)
    res_recv[mine] = res_send[0]
    for number in range(7):
        a, b = row_places[number + 1]
        ref = res_recv.at[a * 2 + lax.div(b, 2)]
        pltpu.make_async_copy(ref, ref, orecv.at[number]).wait()
    for index in range(8):
        xi, k = index // 2, index % 2
        for yi in range(4):
            at = (xi // 2) * 2048 + yi * 512 + (xi % 2) * 256 + k * 128
            out_ref[:, at : at + 128] = res_recv[index, :, yi * 128 : (yi + 1) * 128].astype(F32)
    for copy in started:
        copy.wait_send()


def on_device(activations, out_grads, proj_in, proj_out, basis_in, basis_out, eigen, doc_ids):
    local_count, tokens, width = activations.shape
    rank = proj_in.shape[1]
    return pl.pallas_call(
        functools.partial(kernel, factor=1.0 / (tokens * rank)),
        out_shape=jax.ShapeDtypeStruct((32, 4096), F32),
        in_specs=[pl.BlockSpec(memory_space=pl.ANY)] * 8,
        out_specs=pl.BlockSpec(memory_space=pltpu.VMEM),
        scratch_shapes=[
            pltpu.VMEM((1024, 4096), BF),
            pltpu.VMEM((1024, 4096), BF),
            pltpu.VMEM((64, 4096), BF),
            pltpu.VMEM((64, 4096), BF),
            pltpu.VMEM((64, 64), F32),
            pltpu.VMEM((64, 64), F32),
            pltpu.VMEM((64, 64), F32),
            pltpu.SMEM((32,), jnp.int32),
            pltpu.VMEM((256, 4096), BF),
            pltpu.VMEM((1, 4096), F32),
            pltpu.VMEM((8, 32, 4096), BF),
            pltpu.VMEM((16, 32, 4096), BF),
            pltpu.VMEM((8, 32, 512), BF),
            pltpu.VMEM((8, 32, 512), BF),
            pltpu.VMEM((32, 128), jnp.int32),
            pltpu.VMEM((8, 128), jnp.int32),
            pltpu.VMEM((8, 32, 128), jnp.int32),
            pltpu.VMEM((16, 8, 128), jnp.int32),
            pltpu.SemaphoreType.DMA((8,)),
            pltpu.SemaphoreType.DMA((6,)),
            pltpu.SemaphoreType.DMA((88,)),
            pltpu.SemaphoreType.DMA((88,)),
            pltpu.SemaphoreType.DMA((22,)),
            pltpu.SemaphoreType.DMA((22,)),
            pltpu.SemaphoreType.DMA((7,)),
            pltpu.SemaphoreType.DMA((7,)),
        ],
        compiler_params=pltpu.CompilerParams(
            collective_id=0, has_side_effects=True, vmem_limit_bytes=60 << 20
        ),
        name="influence",
    )(
        activations.reshape(-1, width), out_grads.reshape(-1, width),
        proj_in.T, proj_out.T, basis_in, basis_out, eigen, doc_ids,
    )


def solution(mesh):
    return jax.shard_map(
        on_device,
        mesh=mesh,
        in_specs=(
            P(("grp", "mem"), None, None),
            P(("grp", "mem"), None, None),
            P(),
            P(),
            P(),
            P(),
            P(),
            P(("grp", "mem")),
        ),
        out_specs=P(("grp", "mem"), None),
        check_vma=False,
    )
```

```python
import functools

import jax
import jax.numpy as jnp
from jax import lax
from jax.experimental import pallas as pl
from jax.experimental.pallas import tpu as pltpu
from jax.sharding import PartitionSpec as P

damping = 0.1
BF = jnp.bfloat16
F32 = jnp.float32
MESH = pl.DeviceIdType.MESH
NT = (((1,), (1,)), ((), ()))


def dot(a, b):
    return jnp.dot(a, b, preferred_element_type=F32)


def split(value):
    high = value.astype(BF)
    return high, (value - high.astype(F32)).astype(BF)


def kernel(
    act_hbm, grad_hbm, pin_hbm, pout_hbm, bin_hbm, bout_hbm, eig_hbm, ids_hbm, out_ref,
    act, grad, w_in, w_out, b_in, b_out, eig, ids_ref, w_g, scale,
    rowbuf, colbuf, res_send, res_recv, id_col, id_row, row_ids, col_ids,
    dsem, wsem, ssem, rsem, isend, irecv, osend, orecv,
    *, factor,
):
    g = lax.axis_index("grp")
    m = lax.axis_index("mem")
    x = lax.div(g, 4) * 2 + lax.div(m, 8)
    y = lax.rem(g, 4)
    z = lax.rem(lax.div(m, 2), 4)
    c = lax.rem(m, 2)
    odd = lax.rem(z, 2)
    zr = lax.rem(z + 3 + 2 * odd, 4)
    zc = z + 1 - 2 * odd
    xm, xp, x2 = lax.rem(x + 3, 4), lax.rem(x + 1, 4), lax.rem(x + 2, 4)
    ym, yp, y2 = lax.rem(y + 3, 4), lax.rem(y + 1, 4), lax.rem(y + 2, 4)
    oc = 1 - c

    def device(x, y, z, c):
        return (lax.div(x, 2) * 4 + y, lax.rem(x, 2) * 8 + z * 2 + c)

    def slot(y, z, c):
        return y * 4 + lax.rem(z, 2) * 2 + c

    row_places = [(a, b) for b in (z, zr) for a in (x, xm, xp, x2)]
    row_peers = [device(a, y, b, c) for a, b in row_places[1:]]
    col_places = [(a, b) for b in (z, zc) for a in (y, ym, yp, y2)]
    col_peers = [device(x, a, b, c) for a, b in col_places[1:]]
    cross_peers = [device(x, a, b, oc) for a, b in col_places]
    own = slot(y, z, c)

    weights = [
        pltpu.make_async_copy(src, dst, wsem.at[number])
        for number, (src, dst) in enumerate(
            [
                (bout_hbm, b_out), (bin_hbm, b_in), (eig_hbm, eig), (ids_hbm, ids_ref),
                (pin_hbm, w_in), (pout_hbm, w_out),
            ]
        )
    ]
    loads = []
    for part in range(4):
        rows = pl.ds(part * 256, 256)
        loads.append(
            (
                pltpu.make_async_copy(act_hbm.at[rows], act.at[rows], dsem.at[part]),
                pltpu.make_async_copy(grad_hbm.at[rows], grad.at[rows], dsem.at[4 + part]),
            )
        )
    for copy in weights:
        copy.start()
    for copy in loads[0]:
        copy.start()
    barrier = pltpu.get_barrier_semaphore()
    everyone = row_peers + col_peers + cross_peers
    for peer in everyone:
        pl.semaphore_signal(barrier, inc=1, device_id=peer, device_id_type=MESH)

    for copy in weights[:4]:
        copy.wait()
    for copy in loads[1]:
        copy.start()
    zeros = jnp.zeros((64, 64), BF)
    out_high, out_low = split(b_out[...])
    stacked = jnp.concatenate([zeros, out_high, zeros, out_low], axis=0)
    for tile in range(16):
        unit = lax.broadcasted_iota(jnp.int32, (64, 256), 0)
        lane = lax.broadcasted_iota(jnp.int32, (64, 256), 1)
        spread = jnp.where(lax.div(lane, 64) + tile * 4 == unit, 1.0, 0.0).astype(BF)
        w_g[:, tile * 256 : (tile + 1) * 256] = dot(stacked, spread).astype(BF)
    in_high, in_low = split(b_in[...])
    wide_zeros = jnp.zeros((64, 128), BF)
    w_a = jnp.concatenate(
        [
            jnp.concatenate([in_high, in_high], axis=1),
            wide_zeros,
            jnp.concatenate([in_low, in_low], axis=1),
            wide_zeros,
        ],
        axis=0,
    )
    inverse = 1.0 / jnp.sqrt(eig[...] + damping)
    for tile in range(32):
        scale[:, tile * 128 : (tile + 1) * 128] = jnp.concatenate(
            [inverse[2 * tile : 2 * tile + 1], inverse[2 * tile + 1 : 2 * tile + 2]], axis=1
        )
    row_at = lax.broadcasted_iota(jnp.int32, (256, 256), 0)
    col_at = lax.broadcasted_iota(jnp.int32, (256, 256), 1)
    perm = jnp.where(
        lax.rem(row_at, 8) * 32 + lax.div(row_at, 8) == col_at, 1.0, 0.0
    ).astype(BF)

    lane = lax.broadcasted_iota(jnp.int32, (8, 128), 1)
    first = (odd * 2 + c) * 32
    placed = jnp.zeros((8, 128), jnp.int32)
    for example in range(32):
        value = ids_ref[example]
        placed = jnp.where(lane == first + example, value, placed)
        id_col[example : example + 1, :] = jnp.full((1, 128), value, jnp.int32)
    id_row[...] = placed
    row_ids[0] = id_col[...]
    col_ids[own] = placed

    started = []

    def send(src, dst, send_sem, recv_sem, peer):
        copy = pltpu.make_async_remote_copy(
            src_ref=src, dst_ref=dst, send_sem=send_sem, recv_sem=recv_sem,
            device_id=peer, device_id_type=MESH,
        )
        copy.start()
        started.append(copy)

    to = {
        "x+": device(xp, y, z, c), "x-": device(xm, y, z, c),
        "y+": device(x, yp, z, c), "y-": device(x, ym, z, c),
        "zr": device(x, y, zr, c), "zc": device(x, y, zc, c),
        "core": device(x, y, z, oc),
    }
    count = [0]

    def piece(src, dst, number, where):
        send(src, dst, ssem.at[count[0]], rsem.at[number], to[where])
        count[0] += 1

    def row(k, q):
        return rowbuf.at[k, pl.ds(q * 8, 8)]

    def col(index, q):
        return colbuf.at[index, pl.ds(q * 8, 8)]

    col_names = ["own", "ym", "yp", "y2", "zc", "zcym", "zcyp", "zcy2"]
    row_names = ["own", "xm", "xp", "x2", "zr", "zrxm", "zrxp", "zrx2"]

    def row_number(name, q):
        return (row_names.index(name) - 1) * 4 + q

    def col_number(name, q):
        return 28 + (col_names.index(name) - 1) * 4 + q

    def cross_number(name, q):
        return 56 + col_names.index(name) * 4 + q

    slots = {name: slot(a, b, c) for name, (a, b) in zip(col_names, col_places)}
    other = {name: slot(a, b, oc) for name, (a, b) in zip(col_names, col_places)}

    def row_wait(name, q):
        ref = row(row_names.index(name), q)
        pltpu.make_async_copy(ref, ref, rsem.at[row_number(name, q)]).wait()

    def col_wait(name, q):
        ref = col(slots[name], q)
        pltpu.make_async_copy(ref, ref, rsem.at[col_number(name, q)]).wait()

    def cross_wait(name, q):
        ref = col(other[name], q)
        pltpu.make_async_copy(ref, ref, rsem.at[cross_number(name, q)]).wait()

    def row_send(name, q, where, lands):
        src, dst = row(row_names.index(name), q), row(row_names.index(lands), q)
        piece(src, dst, row_number(lands, q), where)

    def col_send(name, q, where, lands):
        ref = col(slots[name], q)
        piece(ref, ref, col_number(lands, q), where)

    def cross_send(name, q):
        ref = col(slots[name], q)
        piece(ref, ref, cross_number(name, q), "core")

    def own_out(q):
        row_send("own", q, "zr", "zr")
        col_send("own", q, "zc", "zc")
        row_send("own", q, "x+", "xm")
        row_send("own", q, "x-", "xp")
        col_send("own", q, "y+", "ym")
        col_send("own", q, "y-", "yp")
        cross_send("own", q)

    def mid_on(q):
        near = ("xm", "x+", "ym", "y+") if q % 2 == 0 else ("xp", "x-", "yp", "y-")
        row_wait(near[0], q)
        row_send(near[0], q, near[1], "x2")
        col_wait(near[2], q)
        col_send(near[2], q, near[3], "y2")
        row_wait("zr", q)
        row_send("zr", q, "x+", "zrxm")
        row_send("zr", q, "x-", "zrxp")
        col_wait("zc", q)
        col_send("zc", q, "y+", "zcym")
        col_send("zc", q, "y-", "zcyp")
        row_wait("xp" if q % 2 == 0 else "xm", q)
        col_wait("yp" if q % 2 == 0 else "ym", q)
        for name in ("zc", "ym", "yp"):
            cross_send(name, q)

    def last_on(q):
        row_wait("x2", q)
        row_send("x2", q, "zr", "zrx2")
        col_wait("y2", q)
        col_send("y2", q, "zc", "zcy2")
        cross_send("y2", q)

    def side_on(q):
        for name in ("zcym", "zcyp"):
            col_wait(name, q)
            cross_send(name, q)
        for name in ("zrxm", "zrxp"):
            row_wait(name, q)

    mirror = [0, 2, 1, 3, 4, 6, 5, 7]
    def project(part, piece_at, pieces):
        rows = pl.ds(part * 256, 256)
        deep = slice(piece_at * 4096 // pieces, (piece_at + 1) * 4096 // pieces)
        return (
            lax.dot_general(act[rows, deep], w_in[:, deep], NT, preferred_element_type=F32),
            lax.dot_general(grad[rows, deep], w_out[:, deep], NT, preferred_element_type=F32),
        )

    for copy in weights[4:] + list(loads[0]):
        copy.wait()
    for copy in loads[2]:
        copy.start()
    sums = project(0, 0, 1)
    pieces = 4
    for part in range(4):
        if part < 3:
            for copy in loads[part + 1]:
                copy.wait()
        if part == 0:
            for copy in loads[3]:
                copy.start()
        projected = jnp.concatenate(sums, axis=1)
        moved = dot(perm, projected.astype(BF)).astype(BF)
        pair = jnp.concatenate([moved, moved], axis=1)
        rotated = dot(pair, w_a)
        twice = jnp.concatenate([rotated, rotated], axis=1)
        sums = None
        for tile in range(16):
            if part < 3 and tile % (16 // pieces) == 0:
                more = project(part + 1, tile * pieces // 16, pieces)
                sums = more if sums is None else (sums[0] + more[0], sums[1] + more[1])
            lanes = slice(tile * 256, (tile + 1) * 256)
            product = dot(pair, w_g[:, lanes]) * twice
            feature = jnp.sum(product.reshape(32, 8, 256), axis=0) * scale[:, lanes]
            feature = feature.astype(BF)
            rowbuf[0, part * 8 : (part + 1) * 8, lanes] = feature
            colbuf[own, part * 8 : (part + 1) * 8, lanes] = feature
        if part == 0:
            pl.semaphore_wait(barrier, len(everyone))
        own_out(part)
        if part == 0:
            for k, peer in enumerate(row_peers, 1):
                at = mirror[k]
                send(id_col, row_ids.at[at], isend.at[k - 1], irecv.at[at - 1], peer)
            for k, peer in enumerate(col_peers, 1):
                send(id_row, col_ids.at[own], isend.at[6 + k], irecv.at[6 + mirror[k]], peer)
            for k, peer in enumerate(cross_peers):
                send(id_row, col_ids.at[own], isend.at[14 + k], irecv.at[14 + mirror[k]], peer)
        if part >= 2:
            mid_on(part - 2)
    mid_on(2)
    last_on(0)
    mid_on(3)
    last_on(1)
    side_on(0)
    side_on(1)
    last_on(2)
    side_on(2)
    last_on(3)
    side_on(3)
    for q in range(4):
        col_wait("zcy2", q)
        cross_send("zcy2", q)
        row_wait("zrx2", q)

    for k in range(1, 8):
        ref = row_ids.at[k]
        pltpu.make_async_copy(ref, ref, irecv.at[k - 1]).wait()
    for k, name in enumerate(col_names):
        if k:
            ref = col_ids.at[slots[name]]
            pltpu.make_async_copy(ref, ref, irecv.at[6 + k]).wait()
        ref = col_ids.at[other[name]]
        pltpu.make_async_copy(ref, ref, irecv.at[14 + k]).wait()
    for name in col_names:
        for q in range(4):
            cross_wait(name, q)

    mine = x * 2 + lax.div(z, 2)
    for half in range(2):
        block = pl.ds(half * 8, 8)
        products = lax.dot_general(
            rowbuf[...].reshape(256, 4096),
            colbuf[block].reshape(256, 4096),
            NT,
            preferred_element_type=F32,
        )
        ids = jnp.concatenate(
            [
                jnp.sum(col_ids[pl.ds(half * 8 + 4 * part, 4)], axis=0)[:1]
                for part in range(2)
            ],
            axis=1,
        )
        for k in range(8):
            part = products[k * 32 : (k + 1) * 32] * factor
            same = jnp.concatenate([row_ids[k], row_ids[k]], axis=1) == ids
            res_send[half, k] = jnp.where(same, 0.0, part).astype(BF)
        for k in (7, 3, 5, 6, 1, 2, 4):
            at = half * 7 + mirror[k] - 1
            send(
                res_send.at[half, k], res_recv.at[half, mine],
                osend.at[half * 7 + k - 1], orecv.at[at], row_peers[k - 1],
            )
        res_recv[half, mine] = res_send[half, 0]
    for half in range(2):
        for k in range(1, 8):
            a, b = row_places[k]
            ref = res_recv.at[half, a * 2 + lax.div(b, 2)]
            pltpu.make_async_copy(ref, ref, orecv.at[half * 7 + k - 1]).wait()
        for index in range(8):
            xi, k = index // 2, index % 2
            for side in range(2):
                yi = half * 2 + side
                at = (xi // 2) * 2048 + yi * 512 + (xi % 2) * 256 + k * 128
                piece_of = res_recv[half, index, :, side * 128 : (side + 1) * 128]
                out_ref[:, at : at + 128] = piece_of.astype(F32)
    for copy in started:
        copy.wait_send()


def on_device(activations, out_grads, proj_in, proj_out, basis_in, basis_out, eigen, doc_ids):
    local_count, tokens, width = activations.shape
    rank = proj_in.shape[1]
    return pl.pallas_call(
        functools.partial(kernel, factor=1.0 / (tokens * rank)),
        out_shape=jax.ShapeDtypeStruct((32, 4096), F32),
        in_specs=[pl.BlockSpec(memory_space=pl.ANY)] * 8,
        out_specs=pl.BlockSpec(memory_space=pltpu.VMEM),
        scratch_shapes=[
            pltpu.VMEM((1024, 4096), BF),
            pltpu.VMEM((1024, 4096), BF),
            pltpu.VMEM((64, 4096), BF),
            pltpu.VMEM((64, 4096), BF),
            pltpu.VMEM((64, 64), F32),
            pltpu.VMEM((64, 64), F32),
            pltpu.VMEM((64, 64), F32),
            pltpu.SMEM((32,), jnp.int32),
            pltpu.VMEM((256, 4096), BF),
            pltpu.VMEM((1, 4096), F32),
            pltpu.VMEM((8, 32, 4096), BF),
            pltpu.VMEM((16, 32, 4096), BF),
            pltpu.VMEM((2, 8, 32, 256), BF),
            pltpu.VMEM((2, 8, 32, 256), BF),
            pltpu.VMEM((32, 128), jnp.int32),
            pltpu.VMEM((8, 128), jnp.int32),
            pltpu.VMEM((8, 32, 128), jnp.int32),
            pltpu.VMEM((16, 8, 128), jnp.int32),
            pltpu.SemaphoreType.DMA((8,)),
            pltpu.SemaphoreType.DMA((6,)),
            pltpu.SemaphoreType.DMA((88,)),
            pltpu.SemaphoreType.DMA((88,)),
            pltpu.SemaphoreType.DMA((22,)),
            pltpu.SemaphoreType.DMA((22,)),
            pltpu.SemaphoreType.DMA((14,)),
            pltpu.SemaphoreType.DMA((14,)),
        ],
        compiler_params=pltpu.CompilerParams(
            collective_id=0, has_side_effects=True, vmem_limit_bytes=54600 << 10
        ),
        name="influence",
    )(
        activations.reshape(-1, width), out_grads.reshape(-1, width),
        proj_in.T, proj_out.T, *[pltpu.with_memory_space_constraint(v, pltpu.MemorySpace.HBM) for v in (basis_in, basis_out, eigen, doc_ids)],
    )


def solution(mesh):
    return jax.shard_map(
        on_device,
        mesh=mesh,
        in_specs=(
            P(("grp", "mem"), None, None),
            P(("grp", "mem"), None, None),
            P(),
            P(),
            P(),
            P(),
            P(),
            P(("grp", "mem")),
        ),
        out_specs=P(("grp", "mem"), None),
        check_vma=False,
    )
```

```python
import functools

import jax
import jax.numpy as jnp
from jax import lax
from jax.experimental import pallas as pl
from jax.experimental.pallas import tpu as pltpu
from jax.sharding import PartitionSpec as P

damping = 0.1
BF = jnp.bfloat16
F32 = jnp.float32
MESH = pl.DeviceIdType.MESH
NT = (((1,), (1,)), ((), ()))


def dot(a, b):
    return jnp.dot(a, b, preferred_element_type=F32)


def split(value):
    high = value.astype(BF)
    return high, (value - high.astype(F32)).astype(BF)


def kernel(
    act_hbm, grad_hbm, pin_hbm, pout_hbm, bin_hbm, bout_hbm, eig_hbm, ids_hbm, out_ref,
    act, grad, w_in, w_out, b_in, b_out, eig, ids_ref, w_g, scale,
    rowbuf, colbuf, res_send, res_recv, id_row, row_ids, col_ids,
    dsem, wsem, ssem, rsem, isend, irecv, osend, orecv,
    *, factor,
):
    g = lax.axis_index("grp")
    m = lax.axis_index("mem")
    x = lax.div(g, 4) * 2 + lax.div(m, 8)
    y = lax.rem(g, 4)
    z = lax.rem(lax.div(m, 2), 4)
    c = lax.rem(m, 2)
    odd = lax.rem(z, 2)
    zr = lax.rem(z + 3 + 2 * odd, 4)
    zc = z + 1 - 2 * odd
    xm, xp, x2 = lax.rem(x + 3, 4), lax.rem(x + 1, 4), lax.rem(x + 2, 4)
    ym, yp, y2 = lax.rem(y + 3, 4), lax.rem(y + 1, 4), lax.rem(y + 2, 4)
    oc = 1 - c

    def device(x, y, z, c):
        return (lax.div(x, 2) * 4 + y, lax.rem(x, 2) * 8 + z * 2 + c)

    def slot(y, z, c):
        return y * 4 + lax.rem(z, 2) * 2 + c

    row_places = [(a, b) for b in (z, zr) for a in (x, xm, xp, x2)]
    row_peers = [device(a, y, b, c) for a, b in row_places[1:]]
    col_places = [(a, b) for b in (z, zc) for a in (y, ym, yp, y2)]
    col_peers = [device(x, a, b, c) for a, b in col_places[1:]]
    cross_peers = [device(x, a, b, oc) for a, b in col_places]
    own = slot(y, z, c)

    weights = [
        pltpu.make_async_copy(src, dst, wsem.at[number])
        for number, (src, dst) in enumerate(
            [
                (bout_hbm, b_out), (bin_hbm, b_in), (eig_hbm, eig), (ids_hbm, ids_ref),
                (pin_hbm, w_in), (pout_hbm, w_out),
            ]
        )
    ]
    loads = []
    for part in range(4):
        rows = pl.ds(part * 256, 256)
        loads.append(
            (
                pltpu.make_async_copy(act_hbm.at[rows], act.at[rows], dsem.at[part]),
                pltpu.make_async_copy(grad_hbm.at[rows], grad.at[rows], dsem.at[4 + part]),
            )
        )
    for copy in weights:
        copy.start()
    for copy in loads[0]:
        copy.start()
    barrier = pltpu.get_barrier_semaphore()
    everyone = row_peers + col_peers + cross_peers
    for peer in everyone:
        pl.semaphore_signal(barrier, inc=1, device_id=peer, device_id_type=MESH)

    for copy in weights[:4]:
        copy.wait()
    for copy in loads[1]:
        copy.start()
    zeros = jnp.zeros((64, 64), BF)
    out_high, out_low = split(b_out[...])
    stacked = jnp.concatenate([zeros, out_high, zeros, out_low], axis=0)
    for tile in range(16):
        unit = lax.broadcasted_iota(jnp.int32, (64, 256), 0)
        lane = lax.broadcasted_iota(jnp.int32, (64, 256), 1)
        spread = jnp.where(lax.div(lane, 64) + tile * 4 == unit, 1.0, 0.0).astype(BF)
        w_g[:, tile * 256 : (tile + 1) * 256] = dot(stacked, spread).astype(BF)
    in_high, in_low = split(b_in[...])
    wide_zeros = jnp.zeros((64, 128), BF)
    w_a = jnp.concatenate(
        [
            jnp.concatenate([in_high, in_high], axis=1),
            wide_zeros,
            jnp.concatenate([in_low, in_low], axis=1),
            wide_zeros,
        ],
        axis=0,
    )
    inverse = 1.0 / jnp.sqrt(eig[...] + damping)
    for tile in range(32):
        scale[:, tile * 128 : (tile + 1) * 128] = jnp.concatenate(
            [inverse[2 * tile : 2 * tile + 1], inverse[2 * tile + 1 : 2 * tile + 2]], axis=1
        )
    row_at = lax.broadcasted_iota(jnp.int32, (256, 256), 0)
    col_at = lax.broadcasted_iota(jnp.int32, (256, 256), 1)
    perm = jnp.where(
        lax.rem(row_at, 8) * 32 + lax.div(row_at, 8) == col_at, 1.0, 0.0
    ).astype(BF)

    lane = lax.broadcasted_iota(jnp.int32, (8, 128), 1)
    first = (odd * 2 + c) * 32
    placed = jnp.zeros((8, 128), jnp.int32)
    for example in range(32):
        value = ids_ref[example]
        placed = jnp.where(lane == first + example, value, placed)
    id_row[...] = placed
    row_ids[0] = placed
    col_ids[own] = placed

    started = []

    def send(src, dst, send_sem, recv_sem, peer):
        copy = pltpu.make_async_remote_copy(
            src_ref=src, dst_ref=dst, send_sem=send_sem, recv_sem=recv_sem,
            device_id=peer, device_id_type=MESH,
        )
        copy.start()
        started.append(copy)

    to = {
        "x+": device(xp, y, z, c), "x-": device(xm, y, z, c),
        "y+": device(x, yp, z, c), "y-": device(x, ym, z, c),
        "zr": device(x, y, zr, c), "zc": device(x, y, zc, c),
        "core": device(x, y, z, oc),
    }
    count = [0]

    def piece(src, dst, number, where):
        send(src, dst, ssem.at[count[0]], rsem.at[number], to[where])
        count[0] += 1

    def row(k, q):
        return rowbuf.at[k, pl.ds(q * 8, 8)]

    def col(index, q):
        return colbuf.at[index, pl.ds(q * 8, 8)]

    col_names = ["own", "ym", "yp", "y2", "zc", "zcym", "zcyp", "zcy2"]
    row_names = ["own", "xm", "xp", "x2", "zr", "zrxm", "zrxp", "zrx2"]

    def row_number(name, q):
        return (row_names.index(name) - 1) * 4 + q

    def col_number(name, q):
        return 28 + (col_names.index(name) - 1) * 4 + q

    def cross_number(name, q):
        return 56 + col_names.index(name) * 4 + q

    slots = {name: slot(a, b, c) for name, (a, b) in zip(col_names, col_places)}
    other = {name: slot(a, b, oc) for name, (a, b) in zip(col_names, col_places)}

    def row_wait(name, q):
        ref = row(row_names.index(name), q)
        pltpu.make_async_copy(ref, ref, rsem.at[row_number(name, q)]).wait()

    def col_wait(name, q):
        ref = col(slots[name], q)
        pltpu.make_async_copy(ref, ref, rsem.at[col_number(name, q)]).wait()

    def cross_wait(name, q):
        ref = col(other[name], q)
        pltpu.make_async_copy(ref, ref, rsem.at[cross_number(name, q)]).wait()

    def row_send(name, q, where, lands):
        src, dst = row(row_names.index(name), q), row(row_names.index(lands), q)
        piece(src, dst, row_number(lands, q), where)

    def col_send(name, q, where, lands):
        ref = col(slots[name], q)
        piece(ref, ref, col_number(lands, q), where)

    def cross_send(name, q):
        ref = col(slots[name], q)
        piece(ref, ref, cross_number(name, q), "core")

    def own_out(q):
        row_send("own", q, "zr", "zr")
        col_send("own", q, "zc", "zc")
        row_send("own", q, "x+", "xm")
        row_send("own", q, "x-", "xp")
        col_send("own", q, "y+", "ym")
        col_send("own", q, "y-", "yp")
        cross_send("own", q)

    def far_on(q):
        even = q % 2 == 0
        near = ("xm", "x+", "ym", "y+") if even else ("xp", "x-", "yp", "y-")
        row_wait(near[0], q)
        row_send(near[0], q, near[1], "x2")
        col_wait(near[2], q)
        col_send(near[2], q, near[3], "y2")
        cross_send(near[2], q)

    def z_on(q):
        row_wait("zr", q)
        row_send("zr", q, "x+", "zrxm")
        row_send("zr", q, "x-", "zrxp")
        col_wait("zc", q)
        col_send("zc", q, "y+", "zcym")
        col_send("zc", q, "y-", "zcyp")
        cross_send("zc", q)

    def rest_on(q):
        row_wait("xp" if q % 2 == 0 else "xm", q)
        name = "yp" if q % 2 == 0 else "ym"
        col_wait(name, q)
        cross_send(name, q)

    def last_on(q):
        row_wait("x2", q)
        row_send("x2", q, "zr", "zrx2")
        col_wait("y2", q)
        col_send("y2", q, "zc", "zcy2")
        cross_send("y2", q)

    def side_on(q):
        for name in ("zcym", "zcyp"):
            col_wait(name, q)
            cross_send(name, q)
        for name in ("zrxm", "zrxp"):
            row_wait(name, q)

    mirror = [0, 2, 1, 3, 4, 6, 5, 7]
    def project(part, piece_at, pieces):
        rows = pl.ds(part * 256, 256)
        deep = slice(piece_at * 4096 // pieces, (piece_at + 1) * 4096 // pieces)
        return (
            lax.dot_general(act[rows, deep], w_in[:, deep], NT, preferred_element_type=F32),
            lax.dot_general(grad[rows, deep], w_out[:, deep], NT, preferred_element_type=F32),
        )

    for copy in weights[4:] + list(loads[0]):
        copy.wait()
    for copy in loads[2]:
        copy.start()
    sums = project(0, 0, 1)
    for part in range(4):
        if 0 < part < 3:
            for copy in loads[part + 1]:
                copy.wait()
        projected = jnp.concatenate(sums, axis=1)
        moved = dot(perm, projected.astype(BF)).astype(BF)
        pair = jnp.concatenate([moved, moved], axis=1)
        rotated = dot(pair, w_a)
        twice = jnp.concatenate([rotated, rotated], axis=1)
        if 0 < part < 3:
            sums = project(part + 1, 0, 1)
        if part == 2:
            far_on(0)
            z_on(0)
        for tile in range(16):
            lanes = slice(tile * 256, (tile + 1) * 256)
            product = dot(pair, w_g[:, lanes]) * twice
            feature = jnp.sum(product.reshape(32, 8, 256), axis=0) * scale[:, lanes]
            feature = feature.astype(BF)
            rowbuf[0, part * 8 : (part + 1) * 8, lanes] = feature
            colbuf[own, part * 8 : (part + 1) * 8, lanes] = feature
        if part == 0:
            pl.semaphore_wait(barrier, len(everyone))
        own_out(part)
        if part == 0:
            for k, peer in enumerate(row_peers, 1):
                at = mirror[k]
                send(id_row, row_ids.at[at], isend.at[k - 1], irecv.at[at - 1], peer)
            for k, peer in enumerate(col_peers, 1):
                send(id_row, col_ids.at[own], isend.at[6 + k], irecv.at[6 + mirror[k]], peer)
            for k, peer in enumerate(cross_peers):
                send(id_row, col_ids.at[own], isend.at[14 + k], irecv.at[14 + mirror[k]], peer)
        if part == 0:
            for copy in loads[1]:
                copy.wait()
            for copy in loads[3]:
                copy.start()
            sums = project(1, 0, 1)
        if part == 3:
            far_on(1)
            z_on(1)
    far_on(2)
    rest_on(0)
    rest_on(1)
    far_on(3)
    last_on(0)
    z_on(2)
    last_on(1)
    rest_on(2)
    z_on(3)
    last_on(2)
    rest_on(3)
    last_on(3)
    for q in range(4):
        side_on(q)
        col_wait("zcy2", q)
        cross_send("zcy2", q)
    for q in range(4):
        row_wait("zrx2", q)

    for k in range(1, 8):
        ref = row_ids.at[k]
        pltpu.make_async_copy(ref, ref, irecv.at[k - 1]).wait()
    for k, name in enumerate(col_names):
        if k:
            ref = col_ids.at[slots[name]]
            pltpu.make_async_copy(ref, ref, irecv.at[6 + k]).wait()
        ref = col_ids.at[other[name]]
        pltpu.make_async_copy(ref, ref, irecv.at[14 + k]).wait()
    id_cols = []
    for k in range(8):
        turned = jnp.transpose(jnp.broadcast_to(row_ids[k][:1], (128, 128)))
        parts = [turned[at * 32 : (at + 1) * 32] for at in range(4)]
        id_cols.append((parts[0] + parts[1]) + (parts[2] + parts[3]))
    for name in col_names:
        for q in range(4):
            cross_wait(name, q)

    mine = x * 2 + lax.div(z, 2)
    for half in range(2):
        block = pl.ds(half * 8, 8)
        products = lax.dot_general(
            rowbuf[...].reshape(256, 4096),
            colbuf[block].reshape(256, 4096),
            NT,
            preferred_element_type=F32,
        )
        ids = jnp.concatenate(
            [
                jnp.sum(col_ids[pl.ds(half * 8 + 4 * part, 4)], axis=0)[:1]
                for part in range(2)
            ],
            axis=1,
        )
        for k in range(8):
            part = products[k * 32 : (k + 1) * 32] * factor
            same = jnp.concatenate([id_cols[k], id_cols[k]], axis=1) == ids
            res_send[half, k] = jnp.where(same, 0.0, part).astype(BF)
        for k in (7, 3, 5, 6, 1, 2, 4):
            at = half * 7 + mirror[k] - 1
            send(
                res_send.at[half, k], res_recv.at[half, mine],
                osend.at[half * 7 + k - 1], orecv.at[at], row_peers[k - 1],
            )
        res_recv[half, mine] = res_send[half, 0]
    for half in range(2):
        for k in range(1, 8):
            a, b = row_places[k]
            ref = res_recv.at[half, a * 2 + lax.div(b, 2)]
            pltpu.make_async_copy(ref, ref, orecv.at[half * 7 + k - 1]).wait()
        for index in range(8):
            xi, k = index // 2, index % 2
            for side in range(2):
                yi = half * 2 + side
                at = (xi // 2) * 2048 + yi * 512 + (xi % 2) * 256 + k * 128
                piece_of = res_recv[half, index, :, side * 128 : (side + 1) * 128]
                out_ref[:, at : at + 128] = piece_of.astype(F32)
    for copy in started:
        copy.wait_send()


def on_device(activations, out_grads, proj_in, proj_out, basis_in, basis_out, eigen, doc_ids):
    local_count, tokens, width = activations.shape
    rank = proj_in.shape[1]
    return pl.pallas_call(
        functools.partial(kernel, factor=1.0 / (tokens * rank)),
        out_shape=jax.ShapeDtypeStruct((32, 4096), F32),
        in_specs=[pl.BlockSpec(memory_space=pl.ANY)] * 8,
        out_specs=pl.BlockSpec(memory_space=pltpu.VMEM),
        scratch_shapes=[
            pltpu.VMEM((1024, 4096), BF),
            pltpu.VMEM((1024, 4096), BF),
            pltpu.VMEM((64, 4096), BF),
            pltpu.VMEM((64, 4096), BF),
            pltpu.VMEM((64, 64), F32),
            pltpu.VMEM((64, 64), F32),
            pltpu.VMEM((64, 64), F32),
            pltpu.SMEM((32,), jnp.int32),
            pltpu.VMEM((256, 4096), BF),
            pltpu.VMEM((1, 4096), F32),
            pltpu.VMEM((8, 32, 4096), BF),
            pltpu.VMEM((16, 32, 4096), BF),
            pltpu.VMEM((2, 8, 32, 256), BF),
            pltpu.VMEM((2, 8, 32, 256), BF),
            pltpu.VMEM((8, 128), jnp.int32),
            pltpu.VMEM((8, 8, 128), jnp.int32),
            pltpu.VMEM((16, 8, 128), jnp.int32),
            pltpu.SemaphoreType.DMA((8,)),
            pltpu.SemaphoreType.DMA((6,)),
            pltpu.SemaphoreType.DMA((88,)),
            pltpu.SemaphoreType.DMA((88,)),
            pltpu.SemaphoreType.DMA((22,)),
            pltpu.SemaphoreType.DMA((22,)),
            pltpu.SemaphoreType.DMA((14,)),
            pltpu.SemaphoreType.DMA((14,)),
        ],
        compiler_params=pltpu.CompilerParams(
            collective_id=0, has_side_effects=True, vmem_limit_bytes=54600 << 10
        ),
        name="influence",
    )(
        activations.reshape(-1, width), out_grads.reshape(-1, width),
        proj_in.T, proj_out.T, *[pltpu.with_memory_space_constraint(v, pltpu.MemorySpace.HBM) for v in (basis_in, basis_out, eigen, doc_ids)],
    )


def solution(mesh):
    return jax.shard_map(
        on_device,
        mesh=mesh,
        in_specs=(
            P(("grp", "mem"), None, None),
            P(("grp", "mem"), None, None),
            P(),
            P(),
            P(),
            P(),
            P(),
            P(("grp", "mem")),
        ),
        out_specs=P(("grp", "mem"), None),
        check_vma=False,
    )
```

```python
import functools

import jax
import jax.numpy as jnp
from jax import lax
from jax.experimental import pallas as pl
from jax.experimental.pallas import tpu as pltpu
from jax.sharding import PartitionSpec as P

damping = 0.1
BF = jnp.bfloat16
F32 = jnp.float32
MESH = pl.DeviceIdType.MESH
NT = (((1,), (1,)), ((), ()))


def dot(a, b):
    return jnp.dot(a, b, preferred_element_type=F32)


def split(value):
    high = value.astype(BF)
    return high, (value - high.astype(F32)).astype(BF)


def kernel(
    act_hbm, grad_hbm, pin_hbm, pout_hbm, bin_hbm, bout_hbm, eig_hbm, ids_hbm, out_ref,
    act, grad, w_in, w_out, b_in, b_out, eig, ids_ref, w_g, scale,
    rowbuf, colbuf, res_send, res_recv, id_row, row_ids, col_ids,
    dsem, wsem, ssem, rsem, isend, irecv, osend, orecv,
    *, factor,
):
    g = lax.axis_index("grp")
    m = lax.axis_index("mem")
    x = lax.div(g, 4) * 2 + lax.div(m, 8)
    y = lax.rem(g, 4)
    z = lax.rem(lax.div(m, 2), 4)
    c = lax.rem(m, 2)
    odd = lax.rem(z, 2)
    zr = lax.rem(z + 3 + 2 * odd, 4)
    zc = z + 1 - 2 * odd
    xm, xp, x2 = lax.rem(x + 3, 4), lax.rem(x + 1, 4), lax.rem(x + 2, 4)
    ym, yp, y2 = lax.rem(y + 3, 4), lax.rem(y + 1, 4), lax.rem(y + 2, 4)
    oc = 1 - c

    def device(x, y, z, c):
        return (lax.div(x, 2) * 4 + y, lax.rem(x, 2) * 8 + z * 2 + c)

    def slot(y, z, c):
        return y * 4 + lax.rem(z, 2) * 2 + c

    row_places = [(a, b) for b in (z, zr) for a in (x, xm, xp, x2)]
    row_peers = [device(a, y, b, c) for a, b in row_places[1:]]
    col_places = [(a, b) for b in (z, zc) for a in (y, ym, yp, y2)]
    col_peers = [device(x, a, b, c) for a, b in col_places[1:]]
    cross_peers = [device(x, a, b, oc) for a, b in col_places]
    own = slot(y, z, c)

    weights = [
        pltpu.make_async_copy(src, dst, wsem.at[number])
        for number, (src, dst) in enumerate(
            [
                (bout_hbm, b_out), (bin_hbm, b_in), (eig_hbm, eig), (ids_hbm, ids_ref),
                (pin_hbm, w_in), (pout_hbm, w_out),
            ]
        )
    ]
    loads = []
    for part in range(4):
        rows = pl.ds(part * 256, 256)
        loads.append(
            (
                pltpu.make_async_copy(act_hbm.at[rows], act.at[rows], dsem.at[part]),
                pltpu.make_async_copy(grad_hbm.at[rows], grad.at[rows], dsem.at[4 + part]),
            )
        )
    for copy in weights:
        copy.start()
    for copy in loads[0]:
        copy.start()
    barrier = pltpu.get_barrier_semaphore()
    everyone = row_peers + col_peers + cross_peers
    for peer in everyone:
        pl.semaphore_signal(barrier, inc=1, device_id=peer, device_id_type=MESH)

    for copy in weights[:4]:
        copy.wait()
    for copy in loads[1]:
        copy.start()
    zeros = jnp.zeros((64, 64), BF)
    out_high, out_low = split(b_out[...])
    stacked = jnp.concatenate([zeros, out_high, zeros, out_low], axis=0)
    for tile in range(16):
        unit = lax.broadcasted_iota(jnp.int32, (64, 256), 0)
        lane = lax.broadcasted_iota(jnp.int32, (64, 256), 1)
        spread = jnp.where(lax.div(lane, 64) + tile * 4 == unit, 1.0, 0.0).astype(BF)
        w_g[:, tile * 256 : (tile + 1) * 256] = dot(stacked, spread).astype(BF)
    in_high, in_low = split(b_in[...])
    wide_zeros = jnp.zeros((64, 128), BF)
    w_a = jnp.concatenate(
        [
            jnp.concatenate([in_high, in_high], axis=1),
            wide_zeros,
            jnp.concatenate([in_low, in_low], axis=1),
            wide_zeros,
        ],
        axis=0,
    )
    inverse = 1.0 / jnp.sqrt(eig[...] + damping)
    for tile in range(32):
        scale[:, tile * 128 : (tile + 1) * 128] = jnp.concatenate(
            [inverse[2 * tile : 2 * tile + 1], inverse[2 * tile + 1 : 2 * tile + 2]], axis=1
        )
    row_at = lax.broadcasted_iota(jnp.int32, (256, 256), 0)
    col_at = lax.broadcasted_iota(jnp.int32, (256, 256), 1)
    perm = jnp.where(
        lax.rem(row_at, 8) * 32 + lax.div(row_at, 8) == col_at, 1.0, 0.0
    ).astype(BF)

    lane = lax.broadcasted_iota(jnp.int32, (8, 128), 1)
    first = (odd * 2 + c) * 32
    placed = jnp.zeros((8, 128), jnp.int32)
    for example in range(32):
        value = ids_ref[example]
        placed = jnp.where(lane == first + example, value, placed)
    id_row[...] = placed
    row_ids[0] = placed
    col_ids[own] = placed

    started = []

    def send(src, dst, send_sem, recv_sem, peer):
        copy = pltpu.make_async_remote_copy(
            src_ref=src, dst_ref=dst, send_sem=send_sem, recv_sem=recv_sem,
            device_id=peer, device_id_type=MESH,
        )
        copy.start()
        started.append(copy)

    to = {
        "x+": device(xp, y, z, c), "x-": device(xm, y, z, c),
        "y+": device(x, yp, z, c), "y-": device(x, ym, z, c),
        "zr": device(x, y, zr, c), "zc": device(x, y, zc, c),
        "core": device(x, y, z, oc),
    }
    count = [0]

    def piece(src, dst, number, where):
        send(src, dst, ssem.at[count[0]], rsem.at[number], to[where])
        count[0] += 1

    def row(k, q):
        return rowbuf.at[k, pl.ds(q * 8, 8)]

    def col(index, q):
        return colbuf.at[index, pl.ds(q * 8, 8)]

    col_names = ["own", "ym", "yp", "y2", "zc", "zcym", "zcyp", "zcy2"]
    row_names = ["own", "xm", "xp", "x2", "zr", "zrxm", "zrxp", "zrx2"]

    def row_number(name, q):
        return (row_names.index(name) - 1) * 4 + q

    def col_number(name, q):
        return 28 + (col_names.index(name) - 1) * 4 + q

    def cross_number(name, q):
        return 56 + col_names.index(name) * 4 + q

    slots = {name: slot(a, b, c) for name, (a, b) in zip(col_names, col_places)}
    other = {name: slot(a, b, oc) for name, (a, b) in zip(col_names, col_places)}

    def row_wait(name, q):
        ref = row(row_names.index(name), q)
        pltpu.make_async_copy(ref, ref, rsem.at[row_number(name, q)]).wait()

    def col_wait(name, q):
        ref = col(slots[name], q)
        pltpu.make_async_copy(ref, ref, rsem.at[col_number(name, q)]).wait()

    def cross_wait(name, q):
        ref = col(other[name], q)
        pltpu.make_async_copy(ref, ref, rsem.at[cross_number(name, q)]).wait()

    def row_send(name, q, where, lands):
        src, dst = row(row_names.index(name), q), row(row_names.index(lands), q)
        piece(src, dst, row_number(lands, q), where)

    def col_send(name, q, where, lands):
        ref = col(slots[name], q)
        piece(ref, ref, col_number(lands, q), where)

    def cross_send(name, q):
        ref = col(slots[name], q)
        piece(ref, ref, cross_number(name, q), "core")

    def own_out(q):
        row_send("own", q, "zr", "zr")
        col_send("own", q, "zc", "zc")
        row_send("own", q, "x+", "xm")
        row_send("own", q, "x-", "xp")
        col_send("own", q, "y+", "ym")
        col_send("own", q, "y-", "yp")
        cross_send("own", q)

    def far_on(q):
        even = q % 2 == 0
        near = ("xm", "x+", "ym", "y+") if even else ("xp", "x-", "yp", "y-")
        row_wait(near[0], q)
        row_send(near[0], q, near[1], "x2")
        col_wait(near[2], q)
        col_send(near[2], q, near[3], "y2")
        cross_send(near[2], q)

    def z_on(q):
        row_wait("zr", q)
        row_send("zr", q, "x+", "zrxm")
        row_send("zr", q, "x-", "zrxp")
        col_wait("zc", q)
        col_send("zc", q, "y+", "zcym")
        col_send("zc", q, "y-", "zcyp")
        cross_send("zc", q)

    def rest_on(q):
        row_wait("xp" if q % 2 == 0 else "xm", q)
        name = "yp" if q % 2 == 0 else "ym"
        col_wait(name, q)
        cross_send(name, q)

    def last_on(q):
        row_wait("x2", q)
        row_send("x2", q, "zr", "zrx2")
        col_wait("y2", q)
        col_send("y2", q, "zc", "zcy2")
        cross_send("y2", q)

    def side_on(q):
        for name in ("zcym", "zcyp"):
            col_wait(name, q)
            cross_send(name, q)
        for name in ("zrxm", "zrxp"):
            row_wait(name, q)

    mirror = [0, 2, 1, 3, 4, 6, 5, 7]
    def project(part, piece_at, pieces):
        rows = pl.ds(part * 256, 256)
        deep = slice(piece_at * 4096 // pieces, (piece_at + 1) * 4096 // pieces)
        return (
            lax.dot_general(act[rows, deep], w_in[:, deep], NT, preferred_element_type=F32),
            lax.dot_general(grad[rows, deep], w_out[:, deep], NT, preferred_element_type=F32),
        )

    for copy in weights[4:] + list(loads[0]):
        copy.wait()
    for copy in loads[2]:
        copy.start()
    sums = project(0, 0, 1)
    for part in range(4):
        if 0 < part < 3:
            for copy in loads[part + 1]:
                copy.wait()
        projected = jnp.concatenate(sums, axis=1)
        moved = dot(perm, projected.astype(BF)).astype(BF)
        pair = jnp.concatenate([moved, moved], axis=1)
        rotated = dot(pair, w_a)
        twice = jnp.concatenate([rotated, rotated], axis=1)
        if 0 < part < 3:
            sums = project(part + 1, 0, 1)
        if part == 2:
            far_on(0)
            z_on(0)
        for tile in range(16):
            lanes = slice(tile * 256, (tile + 1) * 256)
            product = dot(pair, w_g[:, lanes]) * twice
            feature = jnp.sum(product.reshape(32, 8, 256), axis=0) * scale[:, lanes]
            feature = feature.astype(BF)
            rowbuf[0, part * 8 : (part + 1) * 8, lanes] = feature
            colbuf[own, part * 8 : (part + 1) * 8, lanes] = feature
        if part == 0:
            pl.semaphore_wait(barrier, len(everyone))
        own_out(part)
        if part == 0:
            for k, peer in enumerate(row_peers, 1):
                at = mirror[k]
                send(id_row, row_ids.at[at], isend.at[k - 1], irecv.at[at - 1], peer)
            for k, peer in enumerate(col_peers, 1):
                send(id_row, col_ids.at[own], isend.at[6 + k], irecv.at[6 + mirror[k]], peer)
            for k, peer in enumerate(cross_peers):
                send(id_row, col_ids.at[own], isend.at[14 + k], irecv.at[14 + mirror[k]], peer)
        if part == 0:
            for copy in loads[1]:
                copy.wait()
            for copy in loads[3]:
                copy.start()
            sums = project(1, 0, 1)
        if part == 3:
            far_on(1)
            z_on(1)
    far_on(2)
    rest_on(0)
    rest_on(1)
    far_on(3)
    last_on(0)
    z_on(2)
    last_on(1)
    rest_on(2)
    z_on(3)
    last_on(2)
    rest_on(3)
    last_on(3)
    for q in range(4):
        side_on(q)
        col_wait("zcy2", q)
        cross_send("zcy2", q)
    for q in range(4):
        row_wait("zrx2", q)

    for k in range(1, 8):
        ref = row_ids.at[k]
        pltpu.make_async_copy(ref, ref, irecv.at[k - 1]).wait()
    for k, name in enumerate(col_names):
        if k:
            ref = col_ids.at[slots[name]]
            pltpu.make_async_copy(ref, ref, irecv.at[6 + k]).wait()
        ref = col_ids.at[other[name]]
        pltpu.make_async_copy(ref, ref, irecv.at[14 + k]).wait()
    id_cols = []
    for k in range(8):
        turned = jnp.transpose(jnp.broadcast_to(row_ids[k][:1], (128, 128)))
        parts = [turned[at * 32 : (at + 1) * 32] for at in range(4)]
        id_cols.append((parts[0] + parts[1]) + (parts[2] + parts[3]))

    mine = x * 2 + lax.div(z, 2)
    sides = (("own", "zc", "ym", "zcym"), ("yp", "zcyp", "y2", "zcy2"))
    groups = ((y, ym), (yp, y2))
    for half in range(2):
        for name in sides[half]:
            for q in range(4):
                cross_wait(name, q)
        blocks = [pl.ds(group * 4, 4) for group in groups[half]]
        products = lax.dot_general(
            rowbuf[...].reshape(256, 4096),
            jnp.concatenate([colbuf[block].reshape(128, 4096) for block in blocks], axis=0),
            NT,
            preferred_element_type=F32,
        )
        ids = jnp.concatenate([jnp.sum(col_ids[block], axis=0)[:1] for block in blocks], axis=1)
        for k in range(8):
            part = products[k * 32 : (k + 1) * 32] * factor
            same = jnp.concatenate([id_cols[k], id_cols[k]], axis=1) == ids
            res_send[half, k] = jnp.where(same, 0.0, part).astype(BF)
        for k in (7, 3, 5, 6, 1, 2, 4):
            at = half * 7 + mirror[k] - 1
            send(
                res_send.at[half, k], res_recv.at[half, mine],
                osend.at[half * 7 + k - 1], orecv.at[at], row_peers[k - 1],
            )
        res_recv[half, mine] = res_send[half, 0]
    for half in range(2):
        for k in range(1, 8):
            a, b = row_places[k]
            ref = res_recv.at[half, a * 2 + lax.div(b, 2)]
            pltpu.make_async_copy(ref, ref, orecv.at[half * 7 + k - 1]).wait()
        for index in range(8):
            xi, k = index // 2, index % 2
            for side in range(2):
                at = groups[half][side] * 512 + (xi // 2) * 2048 + (xi % 2) * 256 + k * 128
                lanes = pl.ds(pl.multiple_of(at, 128), 128)
                piece_of = res_recv[half, index, :, side * 128 : (side + 1) * 128]
                out_ref[:, lanes] = piece_of.astype(F32)
    for copy in started:
        copy.wait_send()


def on_device(activations, out_grads, proj_in, proj_out, basis_in, basis_out, eigen, doc_ids):
    local_count, tokens, width = activations.shape
    rank = proj_in.shape[1]
    return pl.pallas_call(
        functools.partial(kernel, factor=1.0 / (tokens * rank)),
        out_shape=jax.ShapeDtypeStruct((32, 4096), F32),
        in_specs=[pl.BlockSpec(memory_space=pl.ANY)] * 8,
        out_specs=pl.BlockSpec(memory_space=pltpu.VMEM),
        scratch_shapes=[
            pltpu.VMEM((1024, 4096), BF),
            pltpu.VMEM((1024, 4096), BF),
            pltpu.VMEM((64, 4096), BF),
            pltpu.VMEM((64, 4096), BF),
            pltpu.VMEM((64, 64), F32),
            pltpu.VMEM((64, 64), F32),
            pltpu.VMEM((64, 64), F32),
            pltpu.SMEM((32,), jnp.int32),
            pltpu.VMEM((256, 4096), BF),
            pltpu.VMEM((1, 4096), F32),
            pltpu.VMEM((8, 32, 4096), BF),
            pltpu.VMEM((16, 32, 4096), BF),
            pltpu.VMEM((2, 8, 32, 256), BF),
            pltpu.VMEM((2, 8, 32, 256), BF),
            pltpu.VMEM((8, 128), jnp.int32),
            pltpu.VMEM((8, 8, 128), jnp.int32),
            pltpu.VMEM((16, 8, 128), jnp.int32),
            pltpu.SemaphoreType.DMA((8,)),
            pltpu.SemaphoreType.DMA((6,)),
            pltpu.SemaphoreType.DMA((88,)),
            pltpu.SemaphoreType.DMA((88,)),
            pltpu.SemaphoreType.DMA((22,)),
            pltpu.SemaphoreType.DMA((22,)),
            pltpu.SemaphoreType.DMA((14,)),
            pltpu.SemaphoreType.DMA((14,)),
        ],
        compiler_params=pltpu.CompilerParams(
            collective_id=0, has_side_effects=True, vmem_limit_bytes=54600 << 10
        ),
        name="influence",
    )(
        activations.reshape(-1, width), out_grads.reshape(-1, width),
        proj_in.T, proj_out.T, *[pltpu.with_memory_space_constraint(v, pltpu.MemorySpace.HBM) for v in (basis_in, basis_out, eigen, doc_ids)],
    )


def solution(mesh):
    return jax.shard_map(
        on_device,
        mesh=mesh,
        in_specs=(
            P(("grp", "mem"), None, None),
            P(("grp", "mem"), None, None),
            P(),
            P(),
            P(),
            P(),
            P(),
            P(("grp", "mem")),
        ),
        out_specs=P(("grp", "mem"), None),
        check_vma=False,
    )
```

```python
import functools

import jax
import jax.numpy as jnp
from jax import lax
from jax.experimental import pallas as pl
from jax.experimental.pallas import tpu as pltpu
from jax.sharding import PartitionSpec as P

damping = 0.1
BF = jnp.bfloat16
F32 = jnp.float32
MESH = pl.DeviceIdType.MESH
NT = (((1,), (1,)), ((), ()))


def dot(a, b):
    return jnp.dot(a, b, preferred_element_type=F32)


def split(value):
    high = value.astype(BF)
    return high, (value - high.astype(F32)).astype(BF)


def kernel(
    act_hbm, grad_hbm, pin_hbm, pout_hbm, bin_hbm, bout_hbm, eig_hbm, ids_hbm, out_ref,
    act, grad, w_in, w_out, b_in, b_out, eig, ids_ref, w_g, scale,
    rowbuf, colbuf, res_send, res_recv, id_row, row_ids, col_ids,
    dsem, wsem, ssem, rsem, isend, irecv, osend, orecv,
    *, factor,
):
    g = lax.axis_index("grp")
    m = lax.axis_index("mem")
    x = lax.div(g, 4) * 2 + lax.div(m, 8)
    y = lax.rem(g, 4)
    z = lax.rem(lax.div(m, 2), 4)
    c = lax.rem(m, 2)
    odd = lax.rem(z, 2)
    zr = lax.rem(z + 3 + 2 * odd, 4)
    zc = z + 1 - 2 * odd
    xm, xp, x2 = lax.rem(x + 3, 4), lax.rem(x + 1, 4), lax.rem(x + 2, 4)
    ym, yp, y2 = lax.rem(y + 3, 4), lax.rem(y + 1, 4), lax.rem(y + 2, 4)
    oc = 1 - c

    def device(x, y, z, c):
        return (lax.div(x, 2) * 4 + y, lax.rem(x, 2) * 8 + z * 2 + c)

    def slot(y, z, c):
        return y * 4 + lax.rem(z, 2) * 2 + c

    row_places = [(a, b) for b in (z, zr) for a in (x, xm, xp, x2)]
    row_peers = [device(a, y, b, c) for a, b in row_places[1:]]
    col_places = [(a, b) for b in (z, zc) for a in (y, ym, yp, y2)]
    col_peers = [device(x, a, b, c) for a, b in col_places[1:]]
    cross_peers = [device(x, a, b, oc) for a, b in col_places]
    own = slot(y, z, c)

    weights = [
        pltpu.make_async_copy(src, dst, wsem.at[number])
        for number, (src, dst) in enumerate(
            [
                (bout_hbm, b_out), (bin_hbm, b_in), (eig_hbm, eig), (ids_hbm, ids_ref),
                (pin_hbm, w_in), (pout_hbm, w_out),
            ]
        )
    ]
    loads = []
    for part in range(4):
        rows = pl.ds(part * 256, 256)
        loads.append(
            (
                pltpu.make_async_copy(act_hbm.at[rows], act.at[rows], dsem.at[part]),
                pltpu.make_async_copy(grad_hbm.at[rows], grad.at[rows], dsem.at[4 + part]),
            )
        )
    for copy in weights:
        copy.start()
    for copy in loads[0]:
        copy.start()
    barrier = pltpu.get_barrier_semaphore()
    everyone = row_peers + col_peers + cross_peers
    for peer in everyone:
        pl.semaphore_signal(barrier, inc=1, device_id=peer, device_id_type=MESH)

    for copy in weights[:4]:
        copy.wait()
    for copy in loads[1]:
        copy.start()
    zeros = jnp.zeros((64, 64), BF)
    out_high, out_low = split(b_out[...])
    stacked = jnp.concatenate([zeros, out_high, zeros, out_low], axis=0)
    for tile in range(16):
        unit = lax.broadcasted_iota(jnp.int32, (64, 256), 0)
        lane = lax.broadcasted_iota(jnp.int32, (64, 256), 1)
        spread = jnp.where(lax.div(lane, 64) + tile * 4 == unit, 1.0, 0.0).astype(BF)
        w_g[:, tile * 256 : (tile + 1) * 256] = dot(stacked, spread).astype(BF)
    in_high, in_low = split(b_in[...])
    wide_zeros = jnp.zeros((64, 128), BF)
    w_a = jnp.concatenate(
        [
            jnp.concatenate([in_high, in_high], axis=1),
            wide_zeros,
            jnp.concatenate([in_low, in_low], axis=1),
            wide_zeros,
        ],
        axis=0,
    )
    inverse = 1.0 / jnp.sqrt(eig[...] + damping)
    for tile in range(32):
        scale[:, tile * 128 : (tile + 1) * 128] = jnp.concatenate(
            [inverse[2 * tile : 2 * tile + 1], inverse[2 * tile + 1 : 2 * tile + 2]], axis=1
        )
    row_at = lax.broadcasted_iota(jnp.int32, (256, 256), 0)
    col_at = lax.broadcasted_iota(jnp.int32, (256, 256), 1)
    perm = jnp.where(
        lax.rem(row_at, 8) * 32 + lax.div(row_at, 8) == col_at, 1.0, 0.0
    ).astype(BF)

    lane = lax.broadcasted_iota(jnp.int32, (8, 128), 1)
    first = (odd * 2 + c) * 32
    placed = jnp.zeros((8, 128), jnp.int32)
    for example in range(32):
        value = ids_ref[example]
        placed = jnp.where(lane == first + example, value, placed)
    id_row[...] = placed
    row_ids[0] = placed
    col_ids[own] = placed

    started = []

    def send(src, dst, send_sem, recv_sem, peer):
        copy = pltpu.make_async_remote_copy(
            src_ref=src, dst_ref=dst, send_sem=send_sem, recv_sem=recv_sem,
            device_id=peer, device_id_type=MESH,
        )
        copy.start()
        started.append(copy)

    to = {
        "x+": device(xp, y, z, c), "x-": device(xm, y, z, c),
        "y+": device(x, yp, z, c), "y-": device(x, ym, z, c),
        "zr": device(x, y, zr, c), "zc": device(x, y, zc, c),
        "core": device(x, y, z, oc),
    }
    count = [0]

    def piece(src, dst, number, where):
        send(src, dst, ssem.at[count[0]], rsem.at[number], to[where])
        count[0] += 1

    def row(k, q):
        return rowbuf.at[k, pl.ds(q * 8, 8)]

    def col(index, q):
        return colbuf.at[index, pl.ds(q * 8, 8)]

    col_names = ["own", "ym", "yp", "y2", "zc", "zcym", "zcyp", "zcy2"]
    row_names = ["own", "xm", "xp", "x2", "zr", "zrxm", "zrxp", "zrx2"]

    def row_number(name, q):
        return (row_names.index(name) - 1) * 4 + q

    def col_number(name, q):
        return 28 + (col_names.index(name) - 1) * 4 + q

    def cross_number(name, q):
        return 56 + col_names.index(name) * 4 + q

    slots = {name: slot(a, b, c) for name, (a, b) in zip(col_names, col_places)}
    other = {name: slot(a, b, oc) for name, (a, b) in zip(col_names, col_places)}

    def row_wait(name, q):
        ref = row(row_names.index(name), q)
        pltpu.make_async_copy(ref, ref, rsem.at[row_number(name, q)]).wait()

    def col_wait(name, q):
        ref = col(slots[name], q)
        pltpu.make_async_copy(ref, ref, rsem.at[col_number(name, q)]).wait()

    def cross_wait(name, q):
        ref = col(other[name], q)
        pltpu.make_async_copy(ref, ref, rsem.at[cross_number(name, q)]).wait()

    def row_send(name, q, where, lands):
        src, dst = row(row_names.index(name), q), row(row_names.index(lands), q)
        piece(src, dst, row_number(lands, q), where)

    def col_send(name, q, where, lands):
        ref = col(slots[name], q)
        piece(ref, ref, col_number(lands, q), where)

    def cross_send(name, q):
        ref = col(slots[name], q)
        piece(ref, ref, cross_number(name, q), "core")

    def own_out(q):
        row_send("own", q, "zr", "zr")
        col_send("own", q, "zc", "zc")
        row_send("own", q, "x+", "xm")
        row_send("own", q, "x-", "xp")
        col_send("own", q, "y+", "ym")
        col_send("own", q, "y-", "yp")
        cross_send("own", q)

    def far_on(q):
        even = q % 2 == 0
        near = ("xm", "x+", "ym", "y+") if even else ("xp", "x-", "yp", "y-")
        row_wait(near[0], q)
        row_send(near[0], q, near[1], "x2")
        col_wait(near[2], q)
        col_send(near[2], q, near[3], "y2")
        cross_send(near[2], q)

    def z_on(q):
        row_wait("zr", q)
        row_send("zr", q, "x+", "zrxm")
        row_send("zr", q, "x-", "zrxp")
        col_wait("zc", q)
        col_send("zc", q, "y+", "zcym")
        col_send("zc", q, "y-", "zcyp")
        cross_send("zc", q)

    def rest_on(q):
        row_wait("xp" if q % 2 == 0 else "xm", q)
        name = "yp" if q % 2 == 0 else "ym"
        col_wait(name, q)
        cross_send(name, q)

    def last_on(q):
        row_wait("x2", q)
        row_send("x2", q, "zr", "zrx2")
        col_wait("y2", q)
        col_send("y2", q, "zc", "zcy2")
        cross_send("y2", q)

    def side_on(q):
        for name in ("zcym", "zcyp"):
            col_wait(name, q)
            cross_send(name, q)
        for name in ("zrxm", "zrxp"):
            row_wait(name, q)

    mirror = [0, 2, 1, 3, 4, 6, 5, 7]
    def project(part, piece_at, pieces):
        rows = pl.ds(part * 256, 256)
        deep = slice(piece_at * 4096 // pieces, (piece_at + 1) * 4096 // pieces)
        return (
            lax.dot_general(act[rows, deep], w_in[:, deep], NT, preferred_element_type=F32),
            lax.dot_general(grad[rows, deep], w_out[:, deep], NT, preferred_element_type=F32),
        )

    for copy in weights[4:] + list(loads[0]):
        copy.wait()
    for copy in loads[2]:
        copy.start()
    sums = project(0, 0, 1)
    for part in range(4):
        if 0 < part < 3:
            for copy in loads[part + 1]:
                copy.wait()
        projected = jnp.concatenate(sums, axis=1)
        moved = dot(perm, projected.astype(BF)).astype(BF)
        pair = jnp.concatenate([moved, moved], axis=1)
        rotated = dot(pair, w_a)
        twice = jnp.concatenate([rotated, rotated], axis=1)
        if 0 < part < 3:
            sums = project(part + 1, 0, 1)
        if part == 2:
            far_on(0)
            z_on(0)
        for tile in range(16):
            lanes = slice(tile * 256, (tile + 1) * 256)
            product = dot(pair, w_g[:, lanes]) * twice
            feature = jnp.sum(product.reshape(32, 8, 256), axis=0) * scale[:, lanes]
            feature = feature.astype(BF)
            rowbuf[0, part * 8 : (part + 1) * 8, lanes] = feature
            colbuf[own, part * 8 : (part + 1) * 8, lanes] = feature
        if part == 0:
            pl.semaphore_wait(barrier, len(everyone))
        own_out(part)
        if part == 0:
            for k, peer in enumerate(row_peers, 1):
                at = mirror[k]
                send(id_row, row_ids.at[at], isend.at[k - 1], irecv.at[at - 1], peer)
            for k, peer in enumerate(col_peers, 1):
                send(id_row, col_ids.at[own], isend.at[6 + k], irecv.at[6 + mirror[k]], peer)
            for k, peer in enumerate(cross_peers):
                send(id_row, col_ids.at[own], isend.at[14 + k], irecv.at[14 + mirror[k]], peer)
        if part == 0:
            for copy in loads[1]:
                copy.wait()
            for copy in loads[3]:
                copy.start()
            sums = project(1, 0, 1)
        if part == 3:
            far_on(1)
            z_on(1)
    far_on(2)
    rest_on(0)
    rest_on(1)
    z_on(2)
    last_on(0)
    far_on(3)
    last_on(1)
    rest_on(2)
    z_on(3)
    last_on(2)
    rest_on(3)
    last_on(3)
    for q in range(4):
        side_on(q)
        col_wait("zcy2", q)
        cross_send("zcy2", q)
    for q in range(4):
        row_wait("zrx2", q)

    for k in range(1, 8):
        ref = row_ids.at[k]
        pltpu.make_async_copy(ref, ref, irecv.at[k - 1]).wait()
    for k, name in enumerate(col_names):
        if k:
            ref = col_ids.at[slots[name]]
            pltpu.make_async_copy(ref, ref, irecv.at[6 + k]).wait()
        ref = col_ids.at[other[name]]
        pltpu.make_async_copy(ref, ref, irecv.at[14 + k]).wait()
    id_cols = []
    for k in range(8):
        turned = jnp.transpose(jnp.broadcast_to(row_ids[k][:1], (128, 128)))
        parts = [turned[at * 32 : (at + 1) * 32] for at in range(4)]
        id_cols.append((parts[0] + parts[1]) + (parts[2] + parts[3]))

    mine = x * 2 + lax.div(z, 2)
    sides = (("own", "zc", "ym", "zcym"), ("yp", "zcyp", "y2", "zcy2"))
    groups = ((y, ym), (yp, y2))
    for half in range(2):
        for name in sides[half]:
            for q in range(4):
                cross_wait(name, q)
        blocks = [pl.ds(group * 4, 4) for group in groups[half]]
        products = lax.dot_general(
            rowbuf[...].reshape(256, 4096),
            jnp.concatenate([colbuf[block].reshape(128, 4096) for block in blocks], axis=0),
            NT,
            preferred_element_type=F32,
        )
        ids = jnp.concatenate([jnp.sum(col_ids[block], axis=0)[:1] for block in blocks], axis=1)
        for k in range(8):
            part = products[k * 32 : (k + 1) * 32] * factor
            same = jnp.concatenate([id_cols[k], id_cols[k]], axis=1) == ids
            res_send[half, k] = jnp.where(same, 0.0, part).astype(BF)
        for k in (7, 3, 5, 6, 1, 2, 4):
            at = half * 7 + mirror[k] - 1
            send(
                res_send.at[half, k], res_recv.at[half, mine],
                osend.at[half * 7 + k - 1], orecv.at[at], row_peers[k - 1],
            )
        res_recv[half, mine] = res_send[half, 0]
    for half in range(2):
        for k in range(1, 8):
            a, b = row_places[k]
            ref = res_recv.at[half, a * 2 + lax.div(b, 2)]
            pltpu.make_async_copy(ref, ref, orecv.at[half * 7 + k - 1]).wait()
        for index in range(8):
            xi, k = index // 2, index % 2
            for side in range(2):
                at = groups[half][side] * 512 + (xi // 2) * 2048 + (xi % 2) * 256 + k * 128
                lanes = pl.ds(pl.multiple_of(at, 128), 128)
                piece_of = res_recv[half, index, :, side * 128 : (side + 1) * 128]
                out_ref[:, lanes] = piece_of.astype(F32)
    for copy in started:
        copy.wait_send()


def on_device(activations, out_grads, proj_in, proj_out, basis_in, basis_out, eigen, doc_ids):
    local_count, tokens, width = activations.shape
    rank = proj_in.shape[1]
    return pl.pallas_call(
        functools.partial(kernel, factor=1.0 / (tokens * rank)),
        out_shape=jax.ShapeDtypeStruct((32, 4096), F32),
        in_specs=[pl.BlockSpec(memory_space=pl.ANY)] * 8,
        out_specs=pl.BlockSpec(memory_space=pltpu.VMEM),
        scratch_shapes=[
            pltpu.VMEM((1024, 4096), BF),
            pltpu.VMEM((1024, 4096), BF),
            pltpu.VMEM((64, 4096), BF),
            pltpu.VMEM((64, 4096), BF),
            pltpu.VMEM((64, 64), F32),
            pltpu.VMEM((64, 64), F32),
            pltpu.VMEM((64, 64), F32),
            pltpu.SMEM((32,), jnp.int32),
            pltpu.VMEM((256, 4096), BF),
            pltpu.VMEM((1, 4096), F32),
            pltpu.VMEM((8, 32, 4096), BF),
            pltpu.VMEM((16, 32, 4096), BF),
            pltpu.VMEM((2, 8, 32, 256), BF),
            pltpu.VMEM((2, 8, 32, 256), BF),
            pltpu.VMEM((8, 128), jnp.int32),
            pltpu.VMEM((8, 8, 128), jnp.int32),
            pltpu.VMEM((16, 8, 128), jnp.int32),
            pltpu.SemaphoreType.DMA((8,)),
            pltpu.SemaphoreType.DMA((6,)),
            pltpu.SemaphoreType.DMA((88,)),
            pltpu.SemaphoreType.DMA((88,)),
            pltpu.SemaphoreType.DMA((22,)),
            pltpu.SemaphoreType.DMA((22,)),
            pltpu.SemaphoreType.DMA((14,)),
            pltpu.SemaphoreType.DMA((14,)),
        ],
        compiler_params=pltpu.CompilerParams(
            collective_id=0, has_side_effects=True, vmem_limit_bytes=54600 << 10
        ),
        name="influence",
    )(
        activations.reshape(-1, width), out_grads.reshape(-1, width),
        proj_in.T, proj_out.T, *[pltpu.with_memory_space_constraint(v, pltpu.MemorySpace.HBM) for v in (basis_in, basis_out, eigen, doc_ids)],
    )


def solution(mesh):
    return jax.shard_map(
        on_device,
        mesh=mesh,
        in_specs=(
            P(("grp", "mem"), None, None),
            P(("grp", "mem"), None, None),
            P(),
            P(),
            P(),
            P(),
            P(),
            P(("grp", "mem")),
        ),
        out_specs=P(("grp", "mem"), None),
        check_vma=False,
    )
```
